32 devices in a mesh: ens: 4 (over y, core), space: 8 (over z, x).
Axes of the slice: x: 2, y: 2, z: 4, core: 2. Of those that a mesh axis runs over, the one named last changes fastest.
Arguments:
- prior_profiles: bfloat16 [128, 64, 64, 128], P('ens', 'space'), may hold values from -6 to 6
- conductivity_profile: bfloat16 [128, 64, 64, 128], P('ens', 'space'), may hold values from 0.5 to 2
- sensor_position_flat: int32 [8192], P('space'), may hold values from 0 to 65535
- observation_slot_count: int32 [8], P('space'), may hold values from 1 to 1024, 5120 in all
- obs_values: float32 [8192], P('space'), may hold values from -6 to 6
- obs_std: float32 [8192], P('space'), may hold values from 0.3 to 3
- obs_noise: float32 [128, 8192], P('ens', 'space'), may hold values from -6 to 6
- params: float32 [128, 2048], P('ens', 'space'), may hold values from -6 to 6
Outputs:
- posterior_parameters: float32 [128, 2048], P('ens', 'space')
- predicted_states: float32 [128, 64, 64, 128], P('ens', 'space')
The draws below stay inside these ranges and needn't reach their ends.
Inputs may be any that keep to these rules, and one draw needn't show every extreme that they name: The live slots of a slab are its first observation_slot_count ones.
All inputs are finite; a program needn't handle non-finite values. No bound on the sum of `observation_slot_count` on one device may be relied on, other than what follows from the above.
Results may differ from the reference program's by a relative error of at most 0.0003.
Values may be sent and summed in bfloat16 or wider, within the bound.
A program may use at most 256 MiB of HBM per device.

```python
import math
import jax
import jax.numpy as jnp
import numpy as np
from jax import lax

M = 128
CZ = 8
NX = 64
NY = 128
NZ = 64
P_SIZE = 2048
OBS_CAP = 1024
OBS = 8192
N_SPACE = 8


def touch_ends(values, key, least, largest):
    spot = [jax.random.randint(jax.random.fold_in(key, axis), (), 0, length) for axis, length in enumerate(values.shape)]
    widest = values.shape.index(max(values.shape))
    beside = spot[:widest] + [(spot[widest] + 1) % values.shape[widest]] + spot[widest + 1:]
    return values.at[tuple(spot)].set(least).at[tuple(beside)].set(largest)


def block_scale(stream_key, shape, cuts, smallest, top_value):
    level = 1.0
    for dim, shards_of in cuts:
        heights = jax.random.uniform(jax.random.fold_in(jax.random.fold_in(stream_key, 6), dim), (shards_of,), jnp.float32, smallest / len(cuts), top_value / len(cuts))
        level = level * jnp.repeat(jnp.exp(heights), shape[dim] // shards_of).reshape((-1,) + (1,) * (len(shape) - 1 - dim))
    return level


def profile(amount, total, limit, lean):
    weights = [(1 << 20) // math.isqrt(standing ** lean) + 1 for standing in range(2, amount + 1)]
    surplus, given = total - limit - (amount - 1), [1] * (amount - 1)
    while surplus > 0:
        movable = [i for i in range(amount - 1) if given[i] < limit]
        mass, left = sum([weights[i] for i in movable]), surplus
        for i in movable:
            addition = min(limit - given[i], max(1, left * weights[i] // mass), surplus)
            given[i] = given[i] + addition
            surplus = surplus - addition
    return np.array([limit] + given)


def ragged(own_key, amount, total, most, slope):
    if amount == 2:
        one = jax.random.randint(own_key, (), max(1, total - most), min(most, total - 1) + 1)
        return jnp.stack([one, total - one])
    sizes = jnp.asarray(profile(amount, total, most, slope), jnp.int32)
    twos = (amount - 1) // 2
    source_of, receiver = sizes[1:1 + 2 * twos:2], sizes[2:2 + 2 * twos:2]
    slack = jnp.minimum(source_of - 1, most - receiver)
    passed = jax.random.randint(jax.random.fold_in(own_key, 1), (twos,), 0, 1 << 20) % (slack + 1)
    sizes = sizes.at[1:1 + 2 * twos:2].set(source_of - passed).at[2:2 + 2 * twos:2].set(receiver + passed)
    return sizes[jax.random.permutation(jax.random.fold_in(own_key, 2), amount)]


def centred(stream_key, shape, width, limit, shards=(), held_as=jnp.bfloat16):
    values = width * jax.random.normal(stream_key, shape, jnp.float32)
    if shards:
        values = values * block_scale(stream_key, shape, shards, -0.22, 0.18)
    return jnp.clip(values, -limit, limit).astype(held_as)


def setup_inputs(seed: int = 0) -> dict:
    seeds = jax.random.split(jax.random.key(seed), 9)
    return {
        "prior_profiles": centred(seeds[0], (M, NZ, NX, NY), 1.0, 6.0, ((0, 4), (1, 8))),
        "conductivity_profile": jnp.clip(jnp.exp(math.log(2.0) - 1.3862944 * jax.random.uniform(seeds[1], (M, NZ, NX, NY), jnp.float32) ** block_scale(seeds[1], (M, NZ, NX, NY), ((0, 4), (1, 8)), -0.2, 0.2)), 0.5, 2.0).astype(jnp.bfloat16),
        "sensor_position_flat": touch_ends(jax.random.randint(seeds[2], (OBS,), 0, CZ * NX * NY), jax.random.fold_in(seeds[2], 1), 0, (CZ * NX * NY) - 1).astype(jnp.int32),
        "observation_slot_count": ragged(seeds[3], N_SPACE, N_SPACE * OBS_CAP * 5 // 8, OBS_CAP, 2).astype(jnp.int32),
        "obs_values": centred(seeds[4], (OBS,), 1.0, 6.0, ((0, 8),), jnp.float32),
        "obs_std": jnp.clip(jnp.exp(math.log(3.0) - 2.3025851 * jax.random.uniform(seeds[5], (OBS,), jnp.float32) ** block_scale(seeds[5], (OBS,), ((0, 8),), -0.2, 0.2)), 0.3, 3.0),
        "obs_noise": centred(seeds[6], (M, OBS), 1.0, 6.0, ((0, 4), (1, 8)), jnp.float32),
        "params": centred(seeds[7], (M, P_SIZE), 1.0, 6.0, ((0, 4), (1, 8)), jnp.float32),
    }


step_size = 0.08

def inner_window(array, starts):
    for dimension in range(3):
        which_axis = array.ndim - 3 + dimension
        extent = array.shape[which_axis] - 2
        array = lax.slice_in_dim(array, starts[dimension], starts[dimension] + extent, axis=which_axis)
    return array

def spread_heat_onestep(field, coeff):
    centre_u = inner_window(field, (1, 1, 1))
    centre_k = inner_window(coeff, (1, 1, 1))
    flux = jnp.zeros_like(centre_u)
    for dimension in range(3):
        for offset in (0, 2):
            starts = [1, 1, 1]
            starts[dimension] = offset
            neigh_u = inner_window(field, tuple(starts))
            neigh_k = inner_window(coeff, tuple(starts))
            flux = flux + 0.5 * (centre_k + neigh_k) * (neigh_u - centre_u)
    return centre_u + step_size * flux

def reference(prior_profiles, conductivity_profile, sensor_position_flat, observation_slot_count, obs_values, obs_std, obs_noise, params):
    cell_table = sensor_position_flat.reshape(N_SPACE, OBS_CAP)

    def realization_march(pair):
        field = jnp.pad(pair[0].astype(jnp.float32), 1)
        coeff = jnp.pad(pair[1].astype(jnp.float32), 1)
        result = spread_heat_onestep(field, coeff)
        slabs = result.reshape(N_SPACE, CZ * NX * NY)
        selected_members = jnp.take_along_axis(slabs, cell_table, axis=1).reshape(OBS)
        return (result, selected_members)
    predicted_states, sampled_readings = lax.map(realization_march, (prior_profiles, conductivity_profile))
    slot_index = jnp.arange(OBS, dtype=jnp.int32) % OBS_CAP
    live_slots = slot_index < jnp.repeat(observation_slot_count, OBS_CAP)
    ens_scale = math.sqrt(M - 1.0)
    centre = lax.optimization_barrier(jnp.mean(sampled_readings, axis=0))
    spread = jnp.where(live_slots, (sampled_readings - centre) / (obs_std * ens_scale), 0.0)
    misfit = jnp.where(live_slots, (obs_values - sampled_readings) / obs_std + obs_noise, 0.0)
    gram_matrix = jnp.dot(spread, spread.T, precision=lax.Precision.HIGHEST)
    cross_term = jnp.dot(spread, misfit.T, precision=lax.Precision.HIGHEST)
    factor = jnp.linalg.cholesky(gram_matrix + jnp.eye(M, dtype=jnp.float32))
    weights = jax.scipy.linalg.cho_solve((factor, True), cross_term)
    anomaly = (params - lax.optimization_barrier(jnp.mean(params, axis=0))) / ens_scale
    posterior_parameters = params + jnp.dot(weights.T, anomaly, precision=lax.Precision.HIGHEST)
    return (posterior_parameters, predicted_states)
```

```python
import functools
import math

import jax
import jax.numpy as jnp
from jax import lax
from jax.experimental import pallas as pl
from jax.experimental.pallas import tpu as pltpu
from jax.sharding import PartitionSpec as P

half_step = 0.04
HI = lax.Precision.HIGHEST
MESH = pl.DeviceIdType.MESH
PARTS = 4


def stencil(u_ref, k_ref, o_ref):
    members, cz, nx, ny = u_ref.shape
    row = lax.broadcasted_iota(jnp.int32, (nx, ny), 0)
    lane = lax.broadcasted_iota(jnp.int32, (nx, ny), 1)
    first_x, last_x = row == 0, row == nx - 1
    first_y, last_y = lane == 0, lane == ny - 1

    def member(m, carry):
        below = None
        u = u_ref[m, 0].astype(jnp.float32)
        k = k_ref[m, 0].astype(jnp.float32)
        for z in range(cz):
            ku = k * u
            fx = (k + pltpu.roll(k, nx - 1, 0)) * (pltpu.roll(u, nx - 1, 0) - u)
            total = jnp.where(last_x, -ku, fx) - jnp.where(first_x, ku, pltpu.roll(fx, 1, 0))
            fy = (k + pltpu.roll(k, ny - 1, 1)) * (pltpu.roll(u, ny - 1, 1) - u)
            total += jnp.where(last_y, -ku, fy) - jnp.where(first_y, ku, pltpu.roll(fy, 1, 1))
            if below is not None:
                total -= below
            if z < cz - 1:
                u_next = u_ref[m, z + 1].astype(jnp.float32)
                k_next = k_ref[m, z + 1].astype(jnp.float32)
                below = (k + k_next) * (u_next - u)
                total += below
            o_ref[m, z * nx : (z + 1) * nx] = u + half_step * total
            if z < cz - 1:
                u, k = u_next, k_next
        return carry

    lax.fori_loop(0, members, member, 0)


def solve(gram_ref, cross_ref, work):
    members = gram_ref.shape[2]
    rows = lax.broadcasted_iota(jnp.int32, (members, members), 0)
    cols = lax.broadcasted_iota(jnp.int32, (members, members), 1)
    lane = lax.broadcasted_iota(jnp.int32, (1, members), 1)
    work[:members] = gram_ref[...].reshape(members, members) + jnp.where(rows == cols, 1.0, 0.0)
    work[members:] = cross_ref[...]

    pivots = 8
    segments = 4
    span = members // segments

    def step(lo, s, diagonal):
        first = lo + s * pivots
        t = work[lo:]
        here = [lane == first + i for i in range(pivots)]
        columns = [
            jnp.sum(jnp.where(here[i], t, 0.0), axis=1, keepdims=True) for i in range(pivots)
        ]
        rows = [work[pl.ds(first + i, 1), :] for i in range(pivots)]
        corner = [
            [jnp.sum(jnp.where(here[j], rows[i], 0.0), axis=1, keepdims=True) for j in range(pivots)]
            for i in range(pivots)
        ]
        for i in range(pivots):
            pivot = corner[i][i]
            diagonal = jnp.where(here[i], pivot, diagonal)
            inverse = 1.0 / pivot
            factor = jnp.where(here[i], 0.0, rows[i] * inverse)
            t = t - columns[i] * factor
            for j in range(i + 1, pivots):
                ratio = corner[i][j] * inverse
                columns[j] = columns[j] - columns[i] * ratio
                rows[j] = rows[j] - corner[j][i] * factor
                for l in range(i + 1, pivots):
                    corner[l][j] = corner[l][j] - corner[l][i] * ratio
        work[lo:] = t
        return diagonal

    diagonal = jnp.ones((1, members), jnp.float32)
    for part in range(segments):
        diagonal = lax.fori_loop(
            0, span // pivots, functools.partial(step, part * span), diagonal
        )
    return work[members:] / diagonal


def analysis_kernel(
    n_e, n_s, pos_ref, count_ref, slots_ref, noise_ref, values_ref, std_ref, params_ref,
    u_hbm, k_hbm,
    pred_hbm, ulo_hbm, klo_hbm, uhi_hbm, khi_hbm, posterior_ref,
    u_ref, k_ref, pred, asked, answer, got, own_at, picked, all_picked, all_params,
    part, parts, total, gram, cross, work,
    load, send_q, recv_q, send_w, recv_w, send_b, recv_b,
    send_a, recv_a, send_h, recv_h, send_p, recv_p, send_s, recv_s, send_g, recv_g,
):
    own, cz, nx, ny = u_ref.shape
    slots = picked.shape[1]
    members = own * n_e
    top = cz - 1
    me_e, me_s = lax.axis_index("ens"), lax.axis_index("space")
    scale = math.sqrt(members - 1.0)
    lo_side, hi_side = me_s > 0, me_s < n_s - 1
    share = own // PARTS

    def local(src, dst, i):
        copy = pltpu.make_async_copy(src, dst, load.at[i])
        copy.start()
        return copy

    loads = [local(u_hbm, u_ref, 0), local(k_hbm, k_ref, 1)]

    def ens_peer(d):
        return (lax.rem(me_e + d, n_e), me_s)

    def space_peer(d):
        return (me_e, lax.rem(me_s + d, n_s))

    barrier = pltpu.get_barrier_semaphore()
    for d in range(1, n_e):
        pl.semaphore_signal(barrier, inc=1, device_id=ens_peer(d), device_id_type=MESH)
    for d in range(1, n_s):
        pl.semaphore_signal(barrier, inc=1, device_id=space_peer(d), device_id_type=MESH)
    pl.semaphore_wait(barrier, n_e + n_s - 2)

    def remote(src, dst, ssem, rsem, peer):
        return pltpu.make_async_remote_copy(
            src_ref=src, dst_ref=dst, send_sem=ssem, recv_sem=rsem,
            device_id=peer, device_id_type=MESH,
        )

    def send(*args):
        copy = remote(*args)
        copy.start()
        return copy

    above, under = (me_e, lax.rem(me_s + 1, n_s)), (me_e, lax.rem(me_s + n_s - 1, n_s))

    def start_pair(pair):
        for side, copies in zip((hi_side, lo_side), pair):
            @pl.when(side)
            def _():
                for copy in copies:
                    copy.start()

    def wait_recv_pair(pair):
        for side, copies in zip((lo_side, hi_side), pair):
            @pl.when(side)
            def _():
                for copy in copies:
                    copy.wait_recv()

    def wait_send_pair(pair):
        for side, copies in zip((hi_side, lo_side), pair):
            @pl.when(side)
            def _():
                for copy in copies:
                    copy.wait_send()

    ask = (
        [remote(slots_ref, asked.at[0], send_q.at[0], recv_q.at[0], above)],
        [remote(slots_ref, asked.at[1], send_q.at[1], recv_q.at[1], under)],
    )
    start_pair(ask)

    def bulk(i):
        at = pl.ds(i * share, share)
        return (
            [
                remote(u_hbm.at[at, top], ulo_hbm.at[at], send_b.at[i, 0], recv_b.at[i, 0], above),
                remote(k_hbm.at[at, top], klo_hbm.at[at], send_b.at[i, 1], recv_b.at[i, 1], above),
            ],
            [
                remote(u_hbm.at[at, 0], uhi_hbm.at[at], send_b.at[i, 2], recv_b.at[i, 2], under),
                remote(k_hbm.at[at, 0], khi_hbm.at[at], send_b.at[i, 3], recv_b.at[i, 3], under),
            ],
        )

    bulks = [bulk(i) for i in range(PARTS)]
    start_pair(bulks[0])
    params_copies = [
        send(params_ref, all_params.at[me_e], send_p.at[d], recv_p.at[d], ens_peer(d))
        for d in range(1, n_e)
    ]
    all_params[me_e] = params_ref[...]

    for copy in loads:
        copy.wait()

    wide = 256
    lane_row = lax.broadcasted_iota(jnp.int32, (ny, wide), 0)
    x_row = lax.broadcasted_iota(jnp.int32, (nx, wide), 0)
    bits_y, bits_x = int(math.log2(ny)), int(math.log2(nx))

    def coordinates(p):
        y = p & (ny - 1)
        x = lax.shift_right_logical(p, bits_y) & (nx - 1)
        return y, x, lax.shift_right_logical(p, bits_y + bits_x)

    wait_recv_pair(ask)
    for e, z in ((1, top), (0, 0)):
        def answer_chunk(c, carry):
            at = pl.ds(pl.multiple_of(c * wide, wide), wide)
            y, x, _ = coordinates(asked[e, :, at])
            hot = jnp.where(lane_row == y, 1.0, 0.0).astype(jnp.bfloat16)
            mask = (x_row == x)[None]
            for f, ref in enumerate((u_ref, k_ref)):
                layer = ref[:, z].reshape(own * nx, ny)
                g = jnp.dot(layer, hot, preferred_element_type=jnp.float32)
                g = jnp.sum(jnp.where(mask, g.reshape(own, nx, wide), 0.0), axis=1)
                answer[e, f, :, at] = g.astype(jnp.bfloat16)
            return carry

        lax.fori_loop(0, slots // wide, answer_chunk, 0)
    reply = (
        [remote(answer.at[1], got.at[0], send_w.at[0], recv_w.at[0], above)],
        [remote(answer.at[0], got.at[1], send_w.at[1], recv_w.at[1], under)],
    )
    start_pair(reply)
    for i in range(1, PARTS - 1):
        start_pair(bulks[i])

    stencil(u_ref, k_ref, pred)
    store = local(pred.at[:, pl.ds(0, cz * nx)], pred_hbm, 2)

    lane = lax.broadcasted_iota(jnp.int32, (own, ny), 1)
    rows = pred.shape[1]
    flat = pred.reshape(own * rows, ny)
    unroll = 32

    def chunk(c, carry):
        def step(s, acc):
            for i in range(unroll):
                jj = s * unroll + i
                p = pos_ref[c * ny + jj]
                at = lax.shift_right_logical(p, bits_y)
                v = flat[pl.ds(at, own, stride=rows), :]
                v = pltpu.roll(v, (jj - p) & (ny - 1), 1)
                acc = jnp.where(lane == jj, v, acc)
            return acc

        acc = lax.fori_loop(0, ny // unroll, step, jnp.zeros((own, ny), jnp.float32))
        picked[:, pl.ds(pl.multiple_of(c * ny, ny), ny)] = acc
        return carry

    lax.fori_loop(0, slots // ny, chunk, 0)

    deep_row = lax.broadcasted_iota(jnp.int32, (2 * ny, wide), 0)

    def own_chunk(c, carry):
        at = pl.ds(pl.multiple_of(c * wide, wide), wide)
        y, x, z = coordinates(slots_ref[:, at])
        spot = jnp.where(z == 0, y, jnp.where(z == top, y + ny, -1))
        hot = jnp.where(deep_row == spot, 1.0, 0.0).astype(jnp.bfloat16)
        mask = (x_row == x)[None]
        for f, ref in enumerate((u_ref, k_ref)):
            layer = jnp.concatenate([ref[:, 0], ref[:, top]], axis=2).reshape(own * nx, 2 * ny)
            g = jnp.dot(layer, hot, preferred_element_type=jnp.float32)
            own_at[f, :, at] = jnp.sum(jnp.where(mask, g.reshape(own, nx, wide), 0.0), axis=1)
        return carry

    lax.fori_loop(0, slots // wide, own_chunk, 0)

    wait_recv_pair(reply)
    _, _, z = coordinates(slots_ref[...])
    u_at, k_at = own_at[0], own_at[1]
    mine = picked[...]
    for e, here, side in ((0, z == 0, lo_side), (1, z == top, hi_side)):
        other = jnp.logical_and(here, side)
        u_n = jnp.where(other, got[e, 0].astype(jnp.float32), 0.0)
        k_n = jnp.where(other, got[e, 1].astype(jnp.float32), 0.0)
        mine = mine + jnp.where(here, half_step * (k_at + k_n) * (u_n - u_at), 0.0)
    picked[...] = mine

    pair = me_e + 1 - 2 * lax.rem(me_e, 2)
    partner = (pair, me_s)
    hops = n_e // 2
    handed = [send(picked, all_picked.at[me_e], send_h.at[0], recv_h.at[0], partner)]
    picked_copies = [
        send(picked, all_picked.at[me_e], send_a.at[d], recv_a.at[d], ens_peer(2 * d))
        for d in range(1, hops)
    ]
    all_picked[me_e] = mine
    live = lax.broadcasted_iota(jnp.int32, (1, slots), 1) < count_ref[0]
    std = std_ref[...]
    inverse = jnp.where(live, 1.0 / (std * scale), 0.0)
    misfit = jnp.where(live, (values_ref[...] - mine) / std + noise_ref[...], 0.0)
    for d in range(1, hops):
        picked_copies[d - 1].wait()
        block = all_picked.at[lax.rem(me_e + n_e - 2 * d, n_e)]
        handed.append(send(block, block, send_h.at[d], recv_h.at[d], partner))
    for copy in handed:
        copy.wait()
    everyone = all_picked[...].reshape(members, slots)
    centre = jnp.sum(everyone, axis=0, keepdims=True) / members
    spread = (everyone - centre) * inverse
    left = jnp.concatenate([(mine - centre) * inverse, misfit], axis=0)
    part[...] = lax.dot_general(
        left, spread, (((1,), (1,)), ((), ())),
        precision=HI, preferred_element_type=jnp.float32,
    )
    space_copies = [
        send(part, parts.at[d], send_s.at[d], recv_s.at[d], space_peer(d)) for d in range(1, n_s)
    ]
    start_pair(bulks[PARTS - 1])
    acc = part[...]
    for d in range(1, n_s):
        space_copies[d - 1].wait()
        acc += parts[d]
    total[...] = acc[:own]
    gram_copies = [
        send(total, gram.at[me_e], send_g.at[d], recv_g.at[d], ens_peer(d))
        for d in range(1, n_e)
    ]
    gram[me_e] = acc[:own]
    cross[...] = acc[own:]
    for copy in gram_copies:
        copy.wait()
    for copy in params_copies:
        copy.wait()
    weights = solve(gram, cross, work)
    everyones = all_params[...].reshape(members, -1)
    centre = jnp.sum(everyones, axis=0, keepdims=True) / members
    anomaly = (everyones - centre) / math.sqrt(members - 1.0)
    posterior_ref[...] = params_ref[...] + jnp.dot(
        weights, anomaly, precision=HI, preferred_element_type=jnp.float32
    )

    store.wait()
    for pair in bulks:
        wait_recv_pair(pair)
    for pair in [ask, reply] + bulks:
        wait_send_pair(pair)


def analysis(n_e, n_s, position, count, noise, values, std, params, u, k):
    own, cz, nx, ny = u.shape
    slots = position.shape[0]
    members = own * n_e
    vmem = pl.BlockSpec(memory_space=pltpu.VMEM)
    smem = pl.BlockSpec(memory_space=pltpu.SMEM)
    whole = pl.BlockSpec(memory_space=pl.ANY)
    dma = pltpu.SemaphoreType.DMA
    f32 = jnp.float32
    layer = jax.ShapeDtypeStruct((own, nx, ny), u.dtype)
    return pl.pallas_call(
        functools.partial(analysis_kernel, n_e, n_s),
        in_specs=[smem, smem] + [vmem] * 5 + [whole] * 2,
        out_specs=[whole] * 5 + [vmem],
        out_shape=[jax.ShapeDtypeStruct((own, cz * nx, ny), f32)]
        + [layer] * 4
        + [jax.ShapeDtypeStruct(params.shape, f32)],
        scratch_shapes=[
            pltpu.VMEM(u.shape, u.dtype),
            pltpu.VMEM(k.shape, k.dtype),
            pltpu.VMEM((own, cz * nx + 8, ny), f32),
            pltpu.VMEM((2, 1, slots), jnp.int32),
            pltpu.VMEM((2, 2, own, slots), u.dtype),
            pltpu.VMEM((2, 2, own, slots), u.dtype),
            pltpu.VMEM((2, own, slots), f32),
            pltpu.VMEM((own, slots), f32),
            pltpu.VMEM((n_e, own, slots), f32),
            pltpu.VMEM((n_e,) + params.shape, f32),
            pltpu.VMEM((2 * own, members), f32),
            pltpu.VMEM((n_s, 2 * own, members), f32),
            pltpu.VMEM((own, members), f32),
            pltpu.VMEM((n_e, own, members), f32),
            pltpu.VMEM((own, members), f32),
            pltpu.VMEM((members + own, members), f32),
            dma((3,)),
        ]
        + [dma((2,))] * 4
        + [dma((PARTS, 4))] * 2
        + [dma((n_e,))] * 6
        + [dma((n_s,))] * 2
        + [dma((n_e,))] * 2,
        compiler_params=pltpu.CompilerParams(collective_id=0, has_side_effects=True),
        name="analysis",
    )(
        position, count, position.reshape(1, -1), noise, values.reshape(1, -1),
        std.reshape(1, -1), params, u, k,
    )


def finish_kernel(
    n_s, pred_ref, ub_ref, kb_ref, ut_ref, kt_ref, ulo_ref, klo_ref, uhi_ref, khi_ref, post_ref,
    o_ref, posterior_ref,
):
    block, cells, ny = pred_ref.shape
    cz, nx = o_ref.shape[1:3]
    me = lax.axis_index("space")
    f32 = jnp.float32
    posterior_ref[...] = post_ref[...]
    for m in range(block):
        for z in range(cz):
            new = pred_ref[m, z * nx : (z + 1) * nx]
            for e, u_ref, k_ref, un_ref, kn_ref, side in (
                (0, ub_ref, kb_ref, ulo_ref, klo_ref, me > 0),
                (cz - 1, ut_ref, kt_ref, uhi_ref, khi_ref, me < n_s - 1),
            ):
                if z == e:
                    un = jnp.where(side, un_ref[m].astype(f32), 0.0)
                    kn = jnp.where(side, kn_ref[m].astype(f32), 0.0)
                    u, k = u_ref[m, 0].astype(f32), k_ref[m, 0].astype(f32)
                    new = new + half_step * (k + kn) * (un - u)
            o_ref[m, z] = new


def finish(n_s, pred, u, k, ulo, klo, uhi, khi, posterior):
    m, cz, nx, ny = u.shape
    block = 4
    low = pl.BlockSpec((block, 1, nx, ny), lambda g: (g, 0, 0, 0))
    high = pl.BlockSpec((block, 1, nx, ny), lambda g: (g, cz - 1, 0, 0))
    halo = pl.BlockSpec((block, nx, ny), lambda g: (g, 0, 0))
    small = pl.BlockSpec(posterior.shape, lambda g: (0, 0))
    return pl.pallas_call(
        functools.partial(finish_kernel, n_s),
        grid=(m // block,),
        in_specs=[pl.BlockSpec((block, cz * nx, ny), lambda g: (g, 0, 0)), low, low, high, high]
        + [halo] * 4
        + [small],
        out_specs=[pl.BlockSpec((block, cz, nx, ny), lambda g: (g, 0, 0, 0)), small],
        out_shape=[
            jax.ShapeDtypeStruct(u.shape, jnp.float32),
            jax.ShapeDtypeStruct(posterior.shape, jnp.float32),
        ],
        name="finish",
    )(pred, u, k, u, k, ulo, klo, uhi, khi, posterior)


def shards(n_e, n_s, u, k, position, count, values, std, noise, params):
    *fields, posterior = analysis(n_e, n_s, position, count, noise, values, std, params, u, k)
    pred, ulo, klo, uhi, khi = fields
    pred, posterior = finish(n_s, pred, u, k, ulo, klo, uhi, khi, posterior)
    return posterior, pred


def solution(mesh):
    in_specs = (
        P("ens", "space", None, None),
        P("ens", "space", None, None),
        P("space"),
        P("space"),
        P("space"),
        P("space"),
        P("ens", "space"),
        P("ens", "space"),
    )
    out_specs = (P("ens", "space"), P("ens", "space", None, None))
    body = functools.partial(shards, mesh.shape["ens"], mesh.shape["space"])
    return jax.shard_map(body, mesh=mesh, in_specs=in_specs, out_specs=out_specs, check_vma=False)
```

```python
import functools
import math

import jax
import jax.numpy as jnp
from jax import lax
from jax.experimental import pallas as pl
from jax.experimental.pallas import tpu as pltpu
from jax.sharding import PartitionSpec as P

half_step = 0.04
HI = lax.Precision.HIGHEST
MESH = pl.DeviceIdType.MESH
VMEM_BYTES = 67043328
PARTS = 4
PAD = 8
WIDE = 256
f32 = jnp.float32
bf16 = jnp.bfloat16


def pad_rows(fu, fk):
    nx = fu.shape[2] - 2 * PAD
    for f in (fu, fk):
        zero = jnp.zeros(f.shape[:2] + (PAD, f.shape[3]), f32)
        f[:, :, :PAD] = zero
        f[:, :, PAD + nx :] = zero


def stencil(lo, hi, u_ref, k_ref, o_ref, fu, fk, fy):
    cz, nx, ny = u_ref.shape[1:]
    group = fu.shape[0]
    r = lax.broadcasted_iota(jnp.int32, (ny, ny), 0)
    c = lax.broadcasted_iota(jnp.int32, (ny, ny), 1)
    eye, following, previous = r == c, r == c + 1, r + 1 == c
    one = lambda mask: jnp.where(mask, 1.0, 0.0)
    plus = [one(following) + one(eye), one(previous) + one(eye)]
    minus = [one(following) - one(eye), one(previous) - one(eye)]
    plus = jnp.concatenate(plus, axis=1).astype(bf16)
    minus = jnp.concatenate(minus, axis=1).astype(bf16)
    span = 32

    def members(i, carry):
        first = lo + i * group
        for w in range(group):
            ks = k_ref[first + w].reshape(cz * nx, ny)
            us = u_ref[first + w].reshape(cz * nx, ny)
            flux = jnp.dot(ks, plus, preferred_element_type=f32) * jnp.dot(
                us, minus, preferred_element_type=f32
            )
            fy[w] = flux[:, :ny] + flux[:, ny:]
            for z in range(cz):
                fu[w, z, PAD : PAD + nx] = u_ref[first + w, z].astype(f32)
                fk[w, z, PAD : PAD + nx] = k_ref[first + w, z].astype(f32)
        for w in range(group):
            for x in range(0, nx, span):
                at = slice(PAD + x, PAD + x + span)
                after = slice(PAD + x + 1, PAD + x + span + 1)
                before = slice(PAD + x - 1, PAD + x + span - 1)
                below = None
                u, k = fu[w, 0, at], fk[w, 0, at]
                for z in range(cz):
                    total = (k + fk[w, z, after]) * (fu[w, z, after] - u)
                    total += (k + fk[w, z, before]) * (fu[w, z, before] - u)
                    total += fy[w, z * nx + x : z * nx + x + span]
                    if below is not None:
                        total -= below
                    if z < cz - 1:
                        u_next, k_next = fu[w, z + 1, at], fk[w, z + 1, at]
                        below = (k + k_next) * (u_next - u)
                        total += below
                    o_ref[first + w, z * nx + x : z * nx + x + span] = u + half_step * total
                    if z < cz - 1:
                        u, k = u_next, k_next
        return carry

    lax.fori_loop(0, (hi - lo) // group, members, 0)


def solve(gram_ref, cross_ref, work):
    members = gram_ref.shape[2]
    rows = lax.broadcasted_iota(jnp.int32, (members, members), 0)
    cols = lax.broadcasted_iota(jnp.int32, (members, members), 1)
    lane = lax.broadcasted_iota(jnp.int32, (1, members), 1)
    work[:members] = gram_ref[...].reshape(members, members) + jnp.where(rows == cols, 1.0, 0.0)
    work[members:] = cross_ref[...]

    pivots = 8
    segments = 4
    span = members // segments

    def step(lo, s, diagonal):
        first = lo + s * pivots
        t = work[lo:]
        here = [lane == first + i for i in range(pivots)]
        columns = [
            jnp.sum(jnp.where(here[i], t, 0.0), axis=1, keepdims=True) for i in range(pivots)
        ]
        rows = [work[pl.ds(first + i, 1), :] for i in range(pivots)]
        corner = [
            [jnp.sum(jnp.where(here[j], rows[i], 0.0), axis=1, keepdims=True) for j in range(pivots)]
            for i in range(pivots)
        ]
        for i in range(pivots):
            pivot = corner[i][i]
            diagonal = jnp.where(here[i], pivot, diagonal)
            inverse = 1.0 / pivot
            factor = jnp.where(here[i], 0.0, rows[i] * inverse)
            t = t - columns[i] * factor
            for j in range(i + 1, pivots):
                ratio = corner[i][j] * inverse
                columns[j] = columns[j] - columns[i] * ratio
                rows[j] = rows[j] - corner[j][i] * factor
                for l in range(i + 1, pivots):
                    corner[l][j] = corner[l][j] - corner[l][i] * ratio
        work[lo:] = t
        return diagonal

    diagonal = jnp.ones((1, members), jnp.float32)
    for part in range(segments):
        diagonal = lax.fori_loop(
            0, span // pivots, functools.partial(step, part * span), diagonal
        )
    return work[members:] / diagonal


def analysis_kernel(
    n_e, n_s, pos_ref, count_ref, slots_hbm, noise_hbm, values_hbm, std_hbm, params_hbm,
    u_hbm, k_hbm,
    pred, posterior_ref,
    u_ref, k_ref, fu, fk, fy, ulo, klo, uhi, khi, flux, back, ret,
    slots_ref, noise_ref, values_ref, std_ref, asked, answer, got, picked, all_picked,
    all_params, part, parts, total, gram, cross, work,
    load, send_q, recv_q, send_w, recv_w, send_b, recv_b, send_r, recv_r,
    send_a, recv_a, send_h, recv_h, send_p, recv_p, send_s, recv_s, send_g, recv_g,
):
    own, cz, nx, ny = u_ref.shape
    slots = slots_ref.shape[1]
    chunks = slots // WIDE
    members = own * n_e
    half = own // 2
    share = half // PARTS
    top = cz - 1
    me_e, me_s = lax.axis_index("ens"), lax.axis_index("space")
    scale = math.sqrt(members - 1.0)
    lo_side, hi_side = me_s > 0, me_s < n_s - 1

    def local(src, dst, i):
        copy = pltpu.make_async_copy(src, dst, load.at[i])
        copy.start()
        return copy

    first, second = pl.ds(0, half), pl.ds(half, half)
    loads = [
        local(u_hbm.at[first], u_ref.at[first], 0),
        local(k_hbm.at[first], k_ref.at[first], 1),
        local(u_hbm.at[second], u_ref.at[second], 2),
        local(k_hbm.at[second], k_ref.at[second], 3),
    ]
    small = [
        local(slots_hbm, slots_ref, 4),
        local(noise_hbm, noise_ref, 5),
        local(values_hbm, values_ref, 6),
        local(std_hbm, std_ref, 7),
        local(params_hbm, all_params.at[me_e], 8),
    ]

    def ens_peer(d):
        return (lax.rem(me_e + d, n_e), me_s)

    def space_peer(d):
        return (me_e, lax.rem(me_s + d, n_s))

    barrier = pltpu.get_barrier_semaphore()
    for d in range(1, n_e):
        pl.semaphore_signal(barrier, inc=1, device_id=ens_peer(d), device_id_type=MESH)
    for d in range(1, n_s):
        pl.semaphore_signal(barrier, inc=1, device_id=space_peer(d), device_id_type=MESH)
    pad_rows(fu, fk)
    pl.semaphore_wait(barrier, n_e + n_s - 2)

    def remote(src, dst, ssem, rsem, peer):
        return pltpu.make_async_remote_copy(
            src_ref=src, dst_ref=dst, send_sem=ssem, recv_sem=rsem,
            device_id=peer, device_id_type=MESH,
        )

    def send(*args):
        copy = remote(*args)
        copy.start()
        return copy

    above, under = (me_e, lax.rem(me_s + 1, n_s)), (me_e, lax.rem(me_s + n_s - 1, n_s))

    def on_sides(sides, pair, what):
        for side, copies in zip(sides, pair):
            @pl.when(side)
            def _():
                for copy in copies:
                    getattr(copy, what)()

    def start_pair(pair):
        on_sides((hi_side, lo_side), pair, "start")

    def wait_send_pair(pair):
        on_sides((hi_side, lo_side), pair, "wait_send")

    def wait_recv_pair(pair):
        on_sides((lo_side, hi_side), pair, "wait_recv")

    ask = (
        [remote(slots_hbm, asked.at[0], send_q.at[0], recv_q.at[0], above)],
        [remote(slots_hbm, asked.at[1], send_q.at[1], recv_q.at[1], under)],
    )
    start_pair(ask)

    def bulk(i):
        at, src_up, src_down = (
            pl.ds(i * share, share), pl.ds(i * share, share), pl.ds(half + i * share, share)
        )
        s, r = send_b.at[i], recv_b.at[i]
        return (
            [
                remote(u_hbm.at[src_up, top], ulo.at[at], s.at[0], r.at[0], above),
                remote(k_hbm.at[src_up, top], klo.at[at], s.at[1], r.at[1], above),
            ],
            [
                remote(u_hbm.at[src_down, 0], uhi.at[at], s.at[2], r.at[2], under),
                remote(k_hbm.at[src_down, 0], khi.at[at], s.at[3], r.at[3], under),
            ],
        )

    def returned(i):
        at = pl.ds(i * share, share)
        s, r = send_r.at[i], recv_r.at[i]
        return (
            [remote(back.at[1, at], ret.at[0, at], s.at[0], r.at[0], above)],
            [remote(back.at[0, at], ret.at[1, at], s.at[1], r.at[1], under)],
        )

    bulks = [bulk(i) for i in range(PARTS)]
    returns = [returned(i) for i in range(PARTS)]

    def border(i):
        wait_recv_pair(bulks[i])

        def one(m, carry):
            for e, z, shift, un_ref, kn_ref, side in (
                (0, 0, 0, ulo, klo, lo_side), (1, top, half, uhi, khi, hi_side),
            ):
                un = jnp.where(side, un_ref[m].astype(f32), 0.0)
                kn = jnp.where(side, kn_ref[m].astype(f32), 0.0)
                u, k = u_ref[m + shift, z].astype(f32), k_ref[m + shift, z].astype(f32)
                value = half_step * (k + kn) * (un - u)
                flux[e, m] = value
                back[e, m] = value.astype(bf16)
            return carry

        lax.fori_loop(i * share, (i + 1) * share, one, 0)
        start_pair(returns[i])

    start_pair(bulks[0])
    start_pair(bulks[1])
    params_copies = [
        send(params_hbm, all_params.at[me_e], send_p.at[d], recv_p.at[d], ens_peer(d))
        for d in range(1, n_e)
    ]

    for copy in loads[:2]:
        copy.wait()
    stencil(0, half, u_ref, k_ref, pred, fu, fk, fy)
    for copy in loads[2:] + small:
        copy.wait()

    lane_row = lax.broadcasted_iota(jnp.int32, (ny, WIDE), 0)
    deep_row = lax.broadcasted_iota(jnp.int32, (2 * ny, WIDE), 0)
    x_row = lax.broadcasted_iota(jnp.int32, (nx, WIDE), 0)
    bits_y, bits_x = int(math.log2(ny)), int(math.log2(nx))

    def coordinates(p):
        y = p & (ny - 1)
        x = lax.shift_right_logical(p, bits_y) & (nx - 1)
        return y, x, lax.shift_right_logical(p, bits_y + bits_x)

    def columns(c):
        return pl.ds(pl.multiple_of(c * WIDE, WIDE), WIDE)

    def pick(layer, hot, mask):
        g = jnp.dot(layer, hot, preferred_element_type=f32)
        return jnp.sum(jnp.where(mask, g.reshape(own, nx, WIDE), 0.0), axis=1)

    wait_recv_pair(ask)
    for e, z in ((1, top), (0, 0)):
        def answer_chunk(c, carry):
            at = columns(c)
            y, x, _ = coordinates(asked[e, :, at])
            hot = jnp.where(lane_row == y, 1.0, 0.0).astype(bf16)
            mask = (x_row == x)[None]
            for f, ref in enumerate((u_ref, k_ref)):
                layer = ref[:, z].reshape(own * nx, ny)
                answer[e, f, :, at] = pick(layer, hot, mask).astype(bf16)
            return carry

        lax.fori_loop(0, chunks, answer_chunk, 0)
    reply = (
        [remote(answer.at[1], got.at[0], send_w.at[0], recv_w.at[0], above)],
        [remote(answer.at[0], got.at[1], send_w.at[1], recv_w.at[1], under)],
    )
    start_pair(reply)
    for i in range(2, PARTS):
        start_pair(bulks[i])
    border(0)
    border(1)
    stencil(half, own, u_ref, k_ref, pred, fu, fk, fy)
    wait_recv_pair(reply)

    lane = lax.broadcasted_iota(jnp.int32, (own, ny), 1)
    rows = pred.shape[1]
    flat = pred.reshape(own * rows, ny)
    pair = me_e + 1 - 2 * lax.rem(me_e, 2)
    partner = (pair, me_s)
    hops = n_e // 2

    def hand(d, c):
        block = all_picked.at[lax.rem(me_e + n_e - 2 * d, n_e), c]
        src = picked.at[c] if d == 0 else block
        return remote(src, block, send_h.at[d, c], recv_h.at[d, c], partner)

    def across(d, c):
        dst = all_picked.at[me_e, c]
        return remote(picked.at[c], dst, send_a.at[d, c], recv_a.at[d, c], ens_peer(2 * d))

    def relay(c):
        for d in range(1, hops):
            across(d, c).wait_recv()
            hand(d, c).start()

    def reading(c, carry):
        at = columns(c)
        y, x, z = coordinates(slots_ref[:, at])
        spot = jnp.where(z == 0, y, jnp.where(z == top, y + ny, -1))
        hot = jnp.where(deep_row == spot, 1.0, 0.0).astype(bf16)
        mask = (x_row == x)[None]
        u_at, k_at = (
            pick(
                jnp.concatenate([ref[:, 0], ref[:, top]], axis=2).reshape(own * nx, 2 * ny),
                hot, mask,
            )
            for ref in (u_ref, k_ref)
        )
        change = jnp.zeros((own, WIDE), f32)
        for e, here, side in ((0, z == 0, lo_side), (1, z == top, hi_side)):
            other = jnp.logical_and(here, side)
            u_n = jnp.where(other, got[e, 0, :, at].astype(f32), 0.0)
            k_n = jnp.where(other, got[e, 1, :, at].astype(f32), 0.0)
            change += jnp.where(here, half_step * (k_at + k_n) * (u_n - u_at), 0.0)
        for h in range(0, WIDE, ny):
            def step(s, acc):
                for i in range(unroll):
                    jj = s * unroll + i
                    p = pos_ref[c * WIDE + h + jj]
                    v = flat[pl.ds(lax.shift_right_logical(p, bits_y), own, stride=rows), :]
                    v = pltpu.roll(v, (jj - p) & (ny - 1), 1)
                    acc = jnp.where(lane == jj, v, acc)
                return acc

            unroll = ny // 2
            acc = lax.fori_loop(0, ny // unroll, step, jnp.zeros((own, ny), f32))
            picked[c, :, h : h + ny] = acc + change[:, h : h + ny]
        all_picked[me_e, c] = picked[c]
        hand(0, c).start()
        for d in range(1, hops):
            across(d, c).start()

        @pl.when(c > 0)
        def _():
            relay(c - 1)

        return carry

    lax.fori_loop(0, chunks, reading, 0)
    border(2)
    relay(chunks - 1)

    part[...] = jnp.zeros_like(part)

    def product(c, carry):
        at = columns(c)
        for d in range(hops):
            hand(d, c).wait_recv()
        mine = picked[c]
        live = lax.broadcasted_iota(jnp.int32, (1, WIDE), 1) + c * WIDE < count_ref[0]
        std = std_ref[:, at]
        inverse = jnp.where(live, 1.0 / (std * scale), 0.0)
        misfit = jnp.where(live, (values_ref[:, at] - mine) / std + noise_ref[:, at], 0.0)
        everyone = all_picked[:, c].reshape(members, WIDE)
        centre = jnp.sum(everyone, axis=0, keepdims=True) / members
        spread = (everyone - centre) * inverse
        left = jnp.concatenate([(mine - centre) * inverse, misfit], axis=0)
        part[...] += lax.dot_general(
            left, spread, (((1,), (1,)), ((), ())),
            precision=HI, preferred_element_type=f32,
        )
        return carry

    lax.fori_loop(0, chunks, product, 0)
    space_copies = [
        send(part, parts.at[d], send_s.at[d], recv_s.at[d], space_peer(d)) for d in range(1, n_s)
    ]
    for i in range(3, PARTS):
        border(i)
    acc = part[...]
    for d in range(1, n_s):
        space_copies[d - 1].wait()
        acc += parts[d]
    total[...] = acc[:own]
    gram_copies = [
        send(total, gram.at[me_e], send_g.at[d], recv_g.at[d], ens_peer(d))
        for d in range(1, n_e)
    ]
    gram[me_e] = acc[:own]
    cross[...] = acc[own:]

    def add_flux(m, carry):
        bottom, upper = pl.ds(0, nx), pl.ds(top * nx, nx)
        pred[m, bottom] = pred[m, bottom] + flux[0, m]
        pred[m + half, upper] = pred[m + half, upper] + flux[1, m]
        return carry

    lax.fori_loop(0, half, add_flux, 0)
    for copy in gram_copies:
        copy.wait()
    for copy in params_copies:
        copy.wait()
    weights = solve(gram, cross, work)
    everyones = all_params[...].reshape(members, -1)
    centre = jnp.sum(everyones, axis=0, keepdims=True) / members
    anomaly = (everyones - centre) / math.sqrt(members - 1.0)
    posterior_ref[...] = all_params[me_e] + jnp.dot(
        weights, anomaly, precision=HI, preferred_element_type=f32
    )

    def add_returned(m, carry):
        for e, z, shift, side in ((0, 0, half, lo_side), (1, top, 0, hi_side)):
            at = pl.ds(z * nx, nx)
            u, k = u_ref[m + shift, z].astype(f32), k_ref[m + shift, z].astype(f32)
            lost = jnp.where(side, ret[e, m].astype(f32), half_step * k * u)
            pred[m + shift, at] = pred[m + shift, at] - lost
        return carry

    for i in range(PARTS):
        wait_recv_pair(returns[i])
        lax.fori_loop(i * share, (i + 1) * share, add_returned, 0)

    for pair in [ask, reply] + bulks + returns:
        wait_send_pair(pair)

    def drain(c, carry):
        for d in range(hops):
            hand(d, c).wait_send()
        for d in range(1, hops):
            across(d, c).wait_send()
        return carry

    lax.fori_loop(0, chunks, drain, 0)


def analysis(n_e, n_s, position, count, noise, values, std, params, u, k):
    own, cz, nx, ny = u.shape
    slots = position.shape[0]
    chunks = slots // WIDE
    members = own * n_e
    half = own // 2
    vmem = pl.BlockSpec(memory_space=pltpu.VMEM)
    smem = pl.BlockSpec(memory_space=pltpu.SMEM)
    hbm = pl.BlockSpec(memory_space=pltpu.HBM)
    dma = pltpu.SemaphoreType.DMA
    field = (own, cz * nx + PAD, ny)
    layers = pltpu.VMEM((half, nx, ny), u.dtype)
    group = 4
    return pl.pallas_call(
        functools.partial(analysis_kernel, n_e, n_s),
        in_specs=[smem, smem] + [hbm] * 7,
        out_specs=[vmem, vmem],
        out_shape=[pltpu.VMEM(field, f32), pltpu.VMEM(params.shape, f32)],
        scratch_shapes=[
            pltpu.VMEM(u.shape, u.dtype),
            pltpu.VMEM(k.shape, k.dtype),
            pltpu.VMEM((group, cz, nx + 2 * PAD, ny), f32),
            pltpu.VMEM((group, cz, nx + 2 * PAD, ny), f32),
            pltpu.VMEM((group, cz * nx, ny), f32),
            layers, layers, layers, layers,
            pltpu.VMEM((2, half, nx, ny), f32),
            pltpu.VMEM((2, half, nx, ny), bf16),
            pltpu.VMEM((2, half, nx, ny), bf16),
            pltpu.VMEM((1, slots), jnp.int32),
            pltpu.VMEM((own, slots), f32),
            pltpu.VMEM((1, slots), f32),
            pltpu.VMEM((1, slots), f32),
            pltpu.VMEM((2, 1, slots), jnp.int32),
            pltpu.VMEM((2, 2, own, slots), bf16),
            pltpu.VMEM((2, 2, own, slots), bf16),
            pltpu.VMEM((chunks, own, WIDE), f32),
            pltpu.VMEM((n_e, chunks, own, WIDE), f32),
            pltpu.VMEM((n_e,) + params.shape, f32),
            pltpu.VMEM((2 * own, members), f32),
            pltpu.VMEM((n_s, 2 * own, members), f32),
            pltpu.VMEM((own, members), f32),
            pltpu.VMEM((n_e, own, members), f32),
            pltpu.VMEM((own, members), f32),
            pltpu.VMEM((members + own, members), f32),
            dma((9,)),
        ]
        + [dma((2,))] * 4
        + [dma((PARTS, 4))] * 2
        + [dma((PARTS, 2))] * 2
        + [dma((n_e // 2, chunks))] * 4
        + [dma((n_e,))] * 2
        + [dma((n_s,))] * 2
        + [dma((n_e,))] * 2,
        compiler_params=pltpu.CompilerParams(
            collective_id=0,
            has_side_effects=True,
            vmem_limit_bytes=VMEM_BYTES - 4 * math.prod(field) - (512 << 10),
        ),
        name="analysis",
    )(
        position, count, position.reshape(1, -1), noise, values.reshape(1, -1),
        std.reshape(1, -1), params, u, k,
    )


def finish_kernel(pred_ref, post_ref, o_ref, posterior_ref, sem):
    members, cz, nx, ny = o_ref.shape
    block = members // sem.shape[0]
    copies = []
    for i in range(sem.shape[0]):
        for z in range(cz):
            at = pl.ds(i * block, block)
            src = pred_ref.at[at, pl.ds(z * nx, nx)]
            copies.append(pltpu.make_async_copy(src, o_ref.at[at, z], sem.at[i, z]))
    for copy in copies:
        copy.start()
    posterior_ref[...] = post_ref[...]
    for copy in copies:
        copy.wait()


def finish(shape, pred, posterior):
    vmem = pl.BlockSpec(memory_space=pltpu.VMEM)
    return pl.pallas_call(
        finish_kernel,
        in_specs=[vmem, vmem],
        out_specs=[pl.BlockSpec(memory_space=pl.ANY), vmem],
        out_shape=[
            jax.ShapeDtypeStruct(shape, jnp.float32),
            jax.ShapeDtypeStruct(posterior.shape, jnp.float32),
        ],
        scratch_shapes=[pltpu.SemaphoreType.DMA((4, shape[1]))],
        compiler_params=pltpu.CompilerParams(vmem_limit_bytes=20 << 20),
        name="finish",
    )(pred, posterior)


def shards(n_e, n_s, u, k, position, count, values, std, noise, params):
    pred, posterior = analysis(n_e, n_s, position, count, noise, values, std, params, u, k)
    pred, posterior = finish(u.shape, pred, posterior)
    return posterior, pred


def solution(mesh):
    in_specs = (
        P("ens", "space", None, None),
        P("ens", "space", None, None),
        P("space"),
        P("space"),
        P("space"),
        P("space"),
        P("ens", "space"),
        P("ens", "space"),
    )
    out_specs = (P("ens", "space"), P("ens", "space", None, None))
    body = functools.partial(shards, mesh.shape["ens"], mesh.shape["space"])
    return jax.shard_map(body, mesh=mesh, in_specs=in_specs, out_specs=out_specs, check_vma=False)
```

```python
import functools
import math

import jax
import jax.numpy as jnp
from jax import lax
from jax.experimental import pallas as pl
from jax.experimental.pallas import tpu as pltpu
from jax.sharding import PartitionSpec as P

half_step = 0.04
HI = lax.Precision.HIGHEST
MESH = pl.DeviceIdType.MESH
VMEM_BYTES = 67043328
PARTS = 4
EARLY = 1
PAD = 8
WIDE = 256
f32 = jnp.float32
bf16 = jnp.bfloat16


def squeeze(f):
    p = f * f
    p = p * p
    p = p * p
    return jnp.where(f < 0.0, -p, p).astype(bf16)


def expand(y):
    y = y.astype(f32)
    root = jnp.sqrt(jnp.sqrt(jnp.sqrt(jnp.abs(y))))
    return jnp.where(y < 0.0, -root, root)


def pad_rows(fu, fk):
    nx = fu.shape[2] - 2 * PAD
    for f in (fu, fk):
        zero = jnp.zeros(f.shape[:2] + (PAD, f.shape[3]), f32)
        f[:, :, :PAD] = zero
        f[:, :, PAD + nx :] = zero


def stencil(lo, hi, u_ref, k_ref, o_ref, fu, fk, fy):
    cz, nx, ny = u_ref.shape[1:]
    group = fu.shape[0]
    r = lax.broadcasted_iota(jnp.int32, (ny, ny), 0)
    c = lax.broadcasted_iota(jnp.int32, (ny, ny), 1)
    eye, following, previous = r == c, r == c + 1, r + 1 == c
    one = lambda mask: jnp.where(mask, 1.0, 0.0)
    plus = [one(following) + one(eye), one(previous) + one(eye)]
    minus = [one(following) - one(eye), one(previous) - one(eye)]
    plus = jnp.concatenate(plus, axis=1).astype(bf16)
    minus = jnp.concatenate(minus, axis=1).astype(bf16)
    span = 32

    def members(i, carry):
        first = lo + i * group
        for w in range(group):
            ks = k_ref[first + w].reshape(cz * nx, ny)
            us = u_ref[first + w].reshape(cz * nx, ny)
            flux = jnp.dot(ks, plus, preferred_element_type=f32) * jnp.dot(
                us, minus, preferred_element_type=f32
            )
            fy[w] = flux[:, :ny] + flux[:, ny:]
            for z in range(cz):
                fu[w, z, PAD : PAD + nx] = u_ref[first + w, z].astype(f32)
                fk[w, z, PAD : PAD + nx] = k_ref[first + w, z].astype(f32)
        for w in range(group):
            for x in range(0, nx, span):
                at = slice(PAD + x, PAD + x + span)
                after = slice(PAD + x + 1, PAD + x + span + 1)
                before = slice(PAD + x - 1, PAD + x + span - 1)
                below = None
                u, k = fu[w, 0, at], fk[w, 0, at]
                for z in range(cz):
                    total = (k + fk[w, z, after]) * (fu[w, z, after] - u)
                    total += (k + fk[w, z, before]) * (fu[w, z, before] - u)
                    total += fy[w, z * nx + x : z * nx + x + span]
                    if below is not None:
                        total -= below
                    if z < cz - 1:
                        u_next, k_next = fu[w, z + 1, at], fk[w, z + 1, at]
                        below = (k + k_next) * (u_next - u)
                        total += below
                    o_ref[first + w, z * nx + x : z * nx + x + span] = u + half_step * total
                    if z < cz - 1:
                        u, k = u_next, k_next
        return carry

    lax.fori_loop(0, (hi - lo) // group, members, 0)


def solve(gram, cross, work):
    members = gram.shape[1]
    rows = lax.broadcasted_iota(jnp.int32, (members, members), 0)
    cols = lax.broadcasted_iota(jnp.int32, (members, members), 1)
    lane = lax.broadcasted_iota(jnp.int32, (1, members), 1)
    work[:members] = gram + jnp.where(rows == cols, 1.0, 0.0)
    work[members:] = cross

    pivots = 8
    segments = 4
    span = members // segments

    def step(lo, s, diagonal):
        first = lo + s * pivots
        t = work[lo:]
        here = [lane == first + i for i in range(pivots)]
        columns = [
            jnp.sum(jnp.where(here[i], t, 0.0), axis=1, keepdims=True) for i in range(pivots)
        ]
        rows = [work[pl.ds(first + i, 1), :] for i in range(pivots)]
        corner = [
            [jnp.sum(jnp.where(here[j], rows[i], 0.0), axis=1, keepdims=True) for j in range(pivots)]
            for i in range(pivots)
        ]
        for i in range(pivots):
            pivot = corner[i][i]
            diagonal = jnp.where(here[i], pivot, diagonal)
            inverse = 1.0 / pivot
            factor = jnp.where(here[i], 0.0, rows[i] * inverse)
            t = t - columns[i] * factor
            for j in range(i + 1, pivots):
                ratio = corner[i][j] * inverse
                columns[j] = columns[j] - columns[i] * ratio
                rows[j] = rows[j] - corner[j][i] * factor
                for l in range(i + 1, pivots):
                    corner[l][j] = corner[l][j] - corner[l][i] * ratio
        work[lo:] = t
        return diagonal

    diagonal = jnp.ones((1, members), jnp.float32)
    for part in range(segments):
        diagonal = lax.fori_loop(
            0, span // pivots, functools.partial(step, part * span), diagonal
        )
    return work[members:] / diagonal


def analysis_kernel(
    n_e, n_s, pos_ref, count_ref, slots_hbm, noise_hbm, values_hbm, std_hbm, params_hbm,
    u_hbm, k_hbm,
    pred, posterior_ref,
    u_ref, k_ref, fu, fk, fy, ulo, klo, uhi, khi, flux, back, ret,
    slots_ref, noise_ref, values_ref, std_ref, asked, answer, got, picked, all_picked,
    all_params, own_at, part, pieces, parts, total, sums, work,
    load, send_q, recv_q, send_w, recv_w, send_b, recv_b, send_r, recv_r,
    send_a, recv_a, send_h, recv_h, send_p, recv_p, send_s, recv_s, send_g, recv_g,
):
    own, cz, nx, ny = u_ref.shape
    slots = slots_ref.shape[1]
    chunks = slots // WIDE
    members = own * n_e
    half = own // 2
    share = half // PARTS
    top = cz - 1
    me_e, me_s = lax.axis_index("ens"), lax.axis_index("space")
    scale = math.sqrt(members - 1.0)
    lo_side, hi_side = me_s > 0, me_s < n_s - 1

    def local(src, dst, i):
        copy = pltpu.make_async_copy(src, dst, load.at[i])
        copy.start()
        return copy

    first, second = pl.ds(0, half), pl.ds(half, half)
    loads = [
        local(u_hbm.at[first], u_ref.at[first], 0),
        local(k_hbm.at[first], k_ref.at[first], 1),
        local(u_hbm.at[second], u_ref.at[second], 2),
        local(k_hbm.at[second], k_ref.at[second], 3),
    ]
    small = [
        local(slots_hbm, slots_ref, 4),
        local(noise_hbm, noise_ref, 5),
        local(values_hbm, values_ref, 6),
        local(std_hbm, std_ref, 7),
        local(params_hbm, all_params.at[me_e], 8),
    ]

    def ens_peer(d):
        return (lax.rem(me_e + d, n_e), me_s)

    def space_peer(d):
        return (me_e, lax.rem(me_s + d, n_s))

    barrier = pltpu.get_barrier_semaphore()
    for d in range(1, n_e):
        pl.semaphore_signal(barrier, inc=1, device_id=ens_peer(d), device_id_type=MESH)
    for d in range(1, n_s):
        pl.semaphore_signal(barrier, inc=1, device_id=space_peer(d), device_id_type=MESH)
    pad_rows(fu, fk)
    pl.semaphore_wait(barrier, n_e + n_s - 2)

    def remote(src, dst, ssem, rsem, peer):
        return pltpu.make_async_remote_copy(
            src_ref=src, dst_ref=dst, send_sem=ssem, recv_sem=rsem,
            device_id=peer, device_id_type=MESH,
        )

    def send(*args):
        copy = remote(*args)
        copy.start()
        return copy

    above, under = (me_e, lax.rem(me_s + 1, n_s)), (me_e, lax.rem(me_s + n_s - 1, n_s))

    def on_sides(sides, pair, what):
        for side, copies in zip(sides, pair):
            @pl.when(side)
            def _():
                for copy in copies:
                    getattr(copy, what)()

    def start_pair(pair):
        on_sides((hi_side, lo_side), pair, "start")

    def wait_send_pair(pair):
        on_sides((hi_side, lo_side), pair, "wait_send")

    def wait_recv_pair(pair):
        on_sides((lo_side, hi_side), pair, "wait_recv")

    ask = (
        [remote(slots_hbm, asked.at[0], send_q.at[0], recv_q.at[0], above)],
        [remote(slots_hbm, asked.at[1], send_q.at[1], recv_q.at[1], under)],
    )
    start_pair(ask)

    def bulk(i):
        at, src_up, src_down = (
            pl.ds(i * share, share), pl.ds(i * share, share), pl.ds(half + i * share, share)
        )
        s, r = send_b.at[i], recv_b.at[i]
        return (
            [
                remote(u_hbm.at[src_up, top], ulo.at[at], s.at[0], r.at[0], above),
                remote(k_hbm.at[src_up, top], klo.at[at], s.at[1], r.at[1], above),
            ],
            [
                remote(u_hbm.at[src_down, 0], uhi.at[at], s.at[2], r.at[2], under),
                remote(k_hbm.at[src_down, 0], khi.at[at], s.at[3], r.at[3], under),
            ],
        )

    def returned(i):
        at = pl.ds(i * share, share)
        s, r = send_r.at[i], recv_r.at[i]
        return (
            [remote(back.at[1, at], ret.at[0, at], s.at[0], r.at[0], above)],
            [remote(back.at[0, at], ret.at[1, at], s.at[1], r.at[1], under)],
        )

    bulks = [bulk(i) for i in range(PARTS)]
    returns = [returned(i) for i in range(PARTS)]

    def border(i):
        wait_recv_pair(bulks[i])

        def one(m, carry):
            for e, z, shift, un_ref, kn_ref, side in (
                (0, 0, 0, ulo, klo, lo_side), (1, top, half, uhi, khi, hi_side),
            ):
                un = jnp.where(side, un_ref[m].astype(f32), 0.0)
                kn = jnp.where(side, kn_ref[m].astype(f32), 0.0)
                u, k = u_ref[m + shift, z].astype(f32), k_ref[m + shift, z].astype(f32)
                value = half_step * (k + kn) * (un - u)
                flux[e, m] = value
                back[e, m] = squeeze(value)
            return carry

        lax.fori_loop(i * share, (i + 1) * share, one, 0)
        start_pair(returns[i])

    for i in range(EARLY):
        start_pair(bulks[i])
    params_copies = [
        send(params_hbm, all_params.at[me_e], send_p.at[d], recv_p.at[d], ens_peer(d))
        for d in range(1, n_e)
    ]

    for copy in loads[:2]:
        copy.wait()
    stencil(0, half // 2, u_ref, k_ref, pred, fu, fk, fy)
    for copy in loads[2:] + small:
        copy.wait()

    lane_row = lax.broadcasted_iota(jnp.int32, (ny, WIDE), 0)
    deep_row = lax.broadcasted_iota(jnp.int32, (2 * ny, WIDE), 0)
    x_row = lax.broadcasted_iota(jnp.int32, (nx, WIDE), 0)
    bits_y, bits_x = int(math.log2(ny)), int(math.log2(nx))

    def coordinates(p):
        y = p & (ny - 1)
        x = lax.shift_right_logical(p, bits_y) & (nx - 1)
        return y, x, lax.shift_right_logical(p, bits_y + bits_x)

    def columns(c):
        return pl.ds(pl.multiple_of(c * WIDE, WIDE), WIDE)

    def pick(layer, hot, mask):
        g = jnp.dot(layer, hot, preferred_element_type=f32)
        return jnp.sum(jnp.where(mask, g.reshape(own, nx, WIDE), 0.0), axis=1)

    reply = (
        [remote(answer.at[1], got.at[0], send_w.at[0], recv_w.at[0], above)],
        [remote(answer.at[0], got.at[1], send_w.at[1], recv_w.at[1], under)],
    )
    wait_recv_pair(ask)
    for e, z in ((1, top), (0, 0)):
        def answer_chunk(c, carry):
            at = columns(c)
            y, x, _ = coordinates(asked[e, :, at])
            hot = jnp.where(lane_row == y, 1.0, 0.0).astype(bf16)
            mask = (x_row == x)[None]
            for f, ref in enumerate((u_ref, k_ref)):
                layer = ref[:, z].reshape(own * nx, ny)
                answer[e, f, :, at] = pick(layer, hot, mask).astype(bf16)
            return carry

        lax.fori_loop(0, chunks, answer_chunk, 0)

        @pl.when((lo_side, hi_side)[e])
        def _():
            reply[1 - e][0].start()

    for i in range(EARLY, PARTS):
        start_pair(bulks[i])
    border(0)
    stencil(half // 2, own, u_ref, k_ref, pred, fu, fk, fy)

    lane = lax.broadcasted_iota(jnp.int32, (own, ny), 1)
    rows = pred.shape[1]
    flat = pred.reshape(own * rows, ny)
    pair = me_e + 1 - 2 * lax.rem(me_e, 2)
    partner = (pair, me_s)
    hops = n_e // 2

    def hand(d, c):
        block = all_picked.at[lax.rem(me_e + n_e - 2 * d, n_e), c]
        src = picked.at[c] if d == 0 else block
        return remote(src, block, send_h.at[d, c], recv_h.at[d, c], partner)

    def across(d, c):
        dst = all_picked.at[me_e, c]
        return remote(picked.at[c], dst, send_a.at[d, c], recv_a.at[d, c], ens_peer(2 * d))

    def relay(c):
        for d in range(1, hops):
            across(d, c).wait_recv()
            hand(d, c).start()

    def reading(c):
        y, x, z = coordinates(slots_ref[:, columns(c)])
        spot = jnp.where(z == 0, y, jnp.where(z == top, y + ny, -1))
        hot = jnp.where(deep_row == spot, 1.0, 0.0).astype(bf16)
        mask = (x_row == x)[None]
        for f, ref in enumerate((u_ref, k_ref)):
            layer = jnp.concatenate([ref[:, 0], ref[:, top]], axis=2)
            own_at[f, c] = pick(layer.reshape(own * nx, 2 * ny), hot, mask)
        for h in range(0, WIDE, ny):
            def step(s, acc):
                for i in range(unroll):
                    jj = s * unroll + i
                    p = pos_ref[c * WIDE + h + jj]
                    v = flat[pl.ds(lax.shift_right_logical(p, bits_y), own, stride=rows), :]
                    v = pltpu.roll(v, (jj - p) & (ny - 1), 1)
                    acc = jnp.where(lane == jj, v, acc)
                return acc

            unroll = ny // 2
            acc = lax.fori_loop(0, ny // unroll, step, jnp.zeros((own, ny), f32))
            picked[c, :, h : h + ny] = acc

    def complete(c):
        at = columns(c)
        _, _, z = coordinates(slots_ref[:, at])
        u_at, k_at = own_at[0, c], own_at[1, c]
        value = picked[c]
        for e, here, side in ((0, z == 0, lo_side), (1, z == top, hi_side)):
            other = jnp.logical_and(here, side)
            u_n = jnp.where(other, got[e, 0, :, at].astype(f32), 0.0)
            k_n = jnp.where(other, got[e, 1, :, at].astype(f32), 0.0)
            value += jnp.where(here, half_step * (k_at + k_n) * (u_n - u_at), 0.0)
        picked[c] = value
        all_picked[me_e, c] = value
        hand(0, c).start()
        for d in range(1, hops):
            across(d, c).start()

    ahead = chunks // 2

    def first_readings(c, carry):
        reading(c)
        return carry

    lax.fori_loop(0, ahead, first_readings, 0)
    wait_recv_pair(reply)

    def more_readings(c, carry):
        complete(c)
        reading(c + ahead)

        @pl.when(c > 0)
        def _():
            relay(c - 1)

        return carry

    lax.fori_loop(0, chunks - ahead, more_readings, 0)
    border(1)

    def last_readings(c, carry):
        complete(c)
        relay(c - 1)
        return carry

    lax.fori_loop(chunks - ahead, chunks, last_readings, 0)
    border(2)
    relay(chunks - 1)

    part[...] = jnp.zeros_like(part)

    def product(c, carry):
        at = columns(c)
        for d in range(hops):
            hand(d, c).wait_recv()
        mine = picked[c]
        live = lax.broadcasted_iota(jnp.int32, (1, WIDE), 1) + c * WIDE < count_ref[0]
        std = std_ref[:, at]
        inverse = jnp.where(live, 1.0 / (std * scale), 0.0)
        misfit = jnp.where(live, (values_ref[:, at] - mine) / std + noise_ref[:, at], 0.0)
        everyone = all_picked[:, c].reshape(members, WIDE)
        centre = jnp.sum(everyone, axis=0, keepdims=True) / members
        spread = (everyone - centre) * inverse
        left = jnp.concatenate([spread, misfit], axis=0)
        part[...] += lax.dot_general(
            left, spread, (((1,), (1,)), ((), ())),
            precision=HI, preferred_element_type=f32,
        )
        return carry

    lax.fori_loop(0, chunks, product, 0)
    grams, crosses = members // n_s, own // n_s
    pieces[:, :grams] = part[:members].reshape(n_s, grams, members)
    for i in range(n_s):
        pieces[i, grams : grams + crosses] = part[members + i * crosses : members + (i + 1) * crosses]
    scatter = []
    for d in range(1, n_s):
        src = pieces.at[lax.rem(me_s + d, n_s)]
        scatter.append(send(src, parts.at[d], send_s.at[d], recv_s.at[d], space_peer(d)))
    for i in range(3, PARTS):
        border(i)
    acc = pieces[me_s]
    for d in range(1, n_s):
        scatter[d - 1].wait()
        acc += parts[d]
    total[...] = acc
    sums[me_s] = acc
    gather = [
        send(total, sums.at[me_s], send_g.at[d], recv_g.at[d], space_peer(d))
        for d in range(1, n_s)
    ]

    def add_flux(m, carry):
        bottom, upper = pl.ds(0, nx), pl.ds(top * nx, nx)
        pred[m, bottom] = pred[m, bottom] + flux[0, m]
        pred[m + half, upper] = pred[m + half, upper] + flux[1, m]
        return carry

    lax.fori_loop(0, half, add_flux, 0)
    for copy in gather:
        copy.wait()
    gram = sums[:, :grams].reshape(members, members)
    cross = jnp.concatenate([sums[i, grams : grams + crosses] for i in range(n_s)], axis=0)
    for copy in params_copies:
        copy.wait()
    weights = solve(gram, cross, work)
    everyones = all_params[...].reshape(members, -1)
    centre = jnp.sum(everyones, axis=0, keepdims=True) / members
    anomaly = (everyones - centre) / math.sqrt(members - 1.0)
    posterior_ref[...] = all_params[me_e] + jnp.dot(
        weights, anomaly, precision=HI, preferred_element_type=f32
    )

    def add_returned(m, carry):
        for e, z, shift, side in ((0, 0, half, lo_side), (1, top, 0, hi_side)):
            at = pl.ds(z * nx, nx)
            u, k = u_ref[m + shift, z].astype(f32), k_ref[m + shift, z].astype(f32)
            lost = jnp.where(side, expand(ret[e, m]), half_step * k * u)
            pred[m + shift, at] = pred[m + shift, at] - lost
        return carry

    for i in range(PARTS):
        wait_recv_pair(returns[i])
        lax.fori_loop(i * share, (i + 1) * share, add_returned, 0)

    for pair in [ask, reply] + bulks + returns:
        wait_send_pair(pair)

    def drain(c, carry):
        for d in range(hops):
            hand(d, c).wait_send()
        for d in range(1, hops):
            across(d, c).wait_send()
        return carry

    lax.fori_loop(0, chunks, drain, 0)


def analysis(n_e, n_s, position, count, noise, values, std, params, u, k):
    own, cz, nx, ny = u.shape
    slots = position.shape[0]
    chunks = slots // WIDE
    members = own * n_e
    half = own // 2
    piece = members // n_s + 8 * pl.cdiv(own // n_s, 8)
    vmem = pl.BlockSpec(memory_space=pltpu.VMEM)
    smem = pl.BlockSpec(memory_space=pltpu.SMEM)
    hbm = pl.BlockSpec(memory_space=pltpu.HBM)
    dma = pltpu.SemaphoreType.DMA
    field = (own, cz * nx + PAD, ny)
    layers = pltpu.VMEM((half, nx, ny), u.dtype)
    group = 4
    return pl.pallas_call(
        functools.partial(analysis_kernel, n_e, n_s),
        in_specs=[smem, smem] + [hbm] * 7,
        out_specs=[vmem, vmem],
        out_shape=[pltpu.VMEM(field, f32), pltpu.VMEM(params.shape, f32)],
        scratch_shapes=[
            pltpu.VMEM(u.shape, u.dtype),
            pltpu.VMEM(k.shape, k.dtype),
            pltpu.VMEM((group, cz, nx + 2 * PAD, ny), f32),
            pltpu.VMEM((group, cz, nx + 2 * PAD, ny), f32),
            pltpu.VMEM((group, cz * nx, ny), f32),
            layers, layers, layers, layers,
            pltpu.VMEM((2, half, nx, ny), f32),
            pltpu.VMEM((2, half, nx, ny), bf16),
            pltpu.VMEM((2, half, nx, ny), bf16),
            pltpu.VMEM((1, slots), jnp.int32),
            pltpu.VMEM((own, slots), f32),
            pltpu.VMEM((1, slots), f32),
            pltpu.VMEM((1, slots), f32),
            pltpu.VMEM((2, 1, slots), jnp.int32),
            pltpu.VMEM((2, 2, own, slots), bf16),
            pltpu.VMEM((2, 2, own, slots), bf16),
            pltpu.VMEM((chunks, own, WIDE), f32),
            pltpu.VMEM((n_e, chunks, own, WIDE), f32),
            pltpu.VMEM((n_e,) + params.shape, f32),
            pltpu.VMEM((2, chunks, own, WIDE), f32),
            pltpu.VMEM((members + own, members), f32),
            pltpu.VMEM((n_s, piece, members), f32),
            pltpu.VMEM((n_s, piece, members), f32),
            pltpu.VMEM((piece, members), f32),
            pltpu.VMEM((n_s, piece, members), f32),
            pltpu.VMEM((members + own, members), f32),
            dma((9,)),
        ]
        + [dma((2,))] * 4
        + [dma((PARTS, 4))] * 2
        + [dma((PARTS, 2))] * 2
        + [dma((n_e // 2, chunks))] * 4
        + [dma((n_e,))] * 2
        + [dma((n_s,))] * 4,
        compiler_params=pltpu.CompilerParams(
            collective_id=0,
            has_side_effects=True,
            vmem_limit_bytes=VMEM_BYTES - 4 * math.prod(field) - (512 << 10),
        ),
        name="analysis",
    )(
        position, count, position.reshape(1, -1), noise, values.reshape(1, -1),
        std.reshape(1, -1), params, u, k,
    )


def finish_kernel(pred_ref, post_ref, o_ref, posterior_ref, sem):
    members, cz, nx, ny = o_ref.shape
    block = members // sem.shape[0]
    copies = []
    for i in range(sem.shape[0]):
        for z in range(cz):
            at = pl.ds(i * block, block)
            src = pred_ref.at[at, pl.ds(z * nx, nx)]
            copies.append(pltpu.make_async_copy(src, o_ref.at[at, z], sem.at[i, z]))
    for copy in copies:
        copy.start()
    posterior_ref[...] = post_ref[...]
    for copy in copies:
        copy.wait()


def finish(shape, pred, posterior):
    vmem = pl.BlockSpec(memory_space=pltpu.VMEM)
    return pl.pallas_call(
        finish_kernel,
        in_specs=[vmem, vmem],
        out_specs=[pl.BlockSpec(memory_space=pl.ANY), vmem],
        out_shape=[
            jax.ShapeDtypeStruct(shape, jnp.float32),
            jax.ShapeDtypeStruct(posterior.shape, jnp.float32),
        ],
        scratch_shapes=[pltpu.SemaphoreType.DMA((4, shape[1]))],
        compiler_params=pltpu.CompilerParams(vmem_limit_bytes=20 << 20),
        name="finish",
    )(pred, posterior)


def shards(n_e, n_s, u, k, position, count, values, std, noise, params):
    pred, posterior = analysis(n_e, n_s, position, count, noise, values, std, params, u, k)
    pred, posterior = finish(u.shape, pred, posterior)
    return posterior, pred


def solution(mesh):
    in_specs = (
        P("ens", "space", None, None),
        P("ens", "space", None, None),
        P("space"),
        P("space"),
        P("space"),
        P("space"),
        P("ens", "space"),
        P("ens", "space"),
    )
    out_specs = (P("ens", "space"), P("ens", "space", None, None))
    body = functools.partial(shards, mesh.shape["ens"], mesh.shape["space"])
    return jax.shard_map(body, mesh=mesh, in_specs=in_specs, out_specs=out_specs, check_vma=False)
```

```python
import functools
import math

import jax
import jax.numpy as jnp
from jax import lax
from jax.experimental import pallas as pl
from jax.experimental.pallas import tpu as pltpu
from jax.sharding import PartitionSpec as P

half_step = 0.04
HI = lax.Precision.HIGHEST
MESH = pl.DeviceIdType.MESH
VMEM_BYTES = 67043328
PARTS = 4
EARLY = 1
LATE = 3
FIRST = 1
BEFORE = 2
AHEAD = 3
MIDDLE = 0
PAD = 8
WIDE = 256
f32 = jnp.float32
bf16 = jnp.bfloat16


def squeeze(f):
    p = f * f
    p = p * p
    p = p * p
    return jnp.where(f < 0.0, -p, p).astype(bf16)


def expand(y):
    y = y.astype(f32)
    root = jnp.sqrt(jnp.sqrt(jnp.sqrt(jnp.abs(y))))
    return jnp.where(y < 0.0, -root, root)


def pad_rows(fu, fk):
    nx = fu.shape[2] - 2 * PAD
    for f in (fu, fk):
        zero = jnp.zeros(f.shape[:2] + (PAD, f.shape[3]), f32)
        f[:, :, :PAD] = zero
        f[:, :, PAD + nx :] = zero


def stencil(lo, hi, u_ref, k_ref, o_ref, fu, fk, fy):
    cz, nx, ny = u_ref.shape[1:]
    group = fu.shape[0]
    r = lax.broadcasted_iota(jnp.int32, (ny, ny), 0)
    c = lax.broadcasted_iota(jnp.int32, (ny, ny), 1)
    eye, following, previous = r == c, r == c + 1, r + 1 == c
    one = lambda mask: jnp.where(mask, 1.0, 0.0)
    plus = [one(following) + one(eye), one(previous) + one(eye)]
    minus = [one(following) - one(eye), one(previous) - one(eye)]
    plus = jnp.concatenate(plus, axis=1).astype(bf16)
    minus = jnp.concatenate(minus, axis=1).astype(bf16)
    span = 32

    def members(i, carry):
        first = lo + i * group
        for w in range(group):
            ks = k_ref[first + w].reshape(cz * nx, ny)
            us = u_ref[first + w].reshape(cz * nx, ny)
            flux = jnp.dot(ks, plus, preferred_element_type=f32) * jnp.dot(
                us, minus, preferred_element_type=f32
            )
            fy[w] = flux[:, :ny] + flux[:, ny:]
            for z in range(cz):
                fu[w, z, PAD : PAD + nx] = u_ref[first + w, z].astype(f32)
                fk[w, z, PAD : PAD + nx] = k_ref[first + w, z].astype(f32)
        for w in range(group):
            for x in range(0, nx, span):
                at = slice(PAD + x, PAD + x + span)
                after = slice(PAD + x + 1, PAD + x + span + 1)
                before = slice(PAD + x - 1, PAD + x + span - 1)
                below = None
                u, k = fu[w, 0, at], fk[w, 0, at]
                for z in range(cz):
                    total = (k + fk[w, z, after]) * (fu[w, z, after] - u)
                    total += (k + fk[w, z, before]) * (fu[w, z, before] - u)
                    total += fy[w, z * nx + x : z * nx + x + span]
                    if below is not None:
                        total -= below
                    if z < cz - 1:
                        u_next, k_next = fu[w, z + 1, at], fk[w, z + 1, at]
                        below = (k + k_next) * (u_next - u)
                        total += below
                    o_ref[first + w, z * nx + x : z * nx + x + span] = u + half_step * total
                    if z < cz - 1:
                        u, k = u_next, k_next
        return carry

    lax.fori_loop(0, (hi - lo) // group, members, 0)


def solve(gram, cross, work):
    members = gram.shape[1]
    rows = lax.broadcasted_iota(jnp.int32, (members, members), 0)
    cols = lax.broadcasted_iota(jnp.int32, (members, members), 1)
    lane = lax.broadcasted_iota(jnp.int32, (1, members), 1)
    work[:members] = gram + jnp.where(rows == cols, 1.0, 0.0)
    work[members:] = cross

    pivots = 8
    segments = 4
    span = members // segments

    def step(lo, s, carry):
        first = lo + s * pivots
        t = work[lo:]
        here = [lane == first + i for i in range(pivots)]
        columns = [
            jnp.sum(jnp.where(here[i], t, 0.0), axis=1, keepdims=True) for i in range(pivots)
        ]
        rows = [work[pl.ds(first + i, 1), :] for i in range(pivots)]
        corner = [
            [jnp.sum(jnp.where(here[j], rows[i], 0.0), axis=1, keepdims=True) for j in range(pivots)]
            for i in range(pivots)
        ]
        rows = [rows[i] - jnp.where(here[i], 1.0, 0.0) for i in range(pivots)]
        for i in range(pivots):
            inverse = 1.0 / corner[i][i]
            rows[i] = rows[i] * inverse
            for j in range(i + 1, pivots):
                corner[i][j] = corner[i][j] * inverse
            for l in range(i + 1, pivots):
                rows[l] = rows[l] - corner[l][i] * rows[i]
                for j in range(i + 1, pivots):
                    corner[l][j] = corner[l][j] - corner[l][i] * corner[i][j]
        for i in range(pivots - 1, -1, -1):
            for j in range(i + 1, pivots):
                rows[i] = rows[i] - corner[i][j] * rows[j]
        for i in range(pivots):
            t = t - columns[i] * rows[i]
        work[lo:] = t
        return carry

    for part in range(segments):
        lax.fori_loop(0, span // pivots, functools.partial(step, part * span), 0)
    return work[members:]


def analysis_kernel(
    n_e, n_s, pos_ref, count_ref, slots_hbm, noise_hbm, values_hbm, std_hbm, params_hbm,
    u_hbm, k_hbm,
    pred, posterior_ref,
    u_ref, k_ref, fu, fk, fy, ulo, klo, uhi, khi, flux, back, ret,
    slots_ref, noise_ref, values_ref, std_ref, asked, answer, got, picked, all_picked,
    all_params, own_at, part, pieces, parts, total, sums, work,
    gate, load, send_q, recv_q, send_w, recv_w, send_b, recv_b, send_r, recv_r,
    send_a, recv_a, send_h, recv_h, send_p, recv_p, send_s, recv_s, send_g, recv_g,
):
    own, cz, nx, ny = u_ref.shape
    slots = slots_ref.shape[1]
    chunks = slots // WIDE
    members = own * n_e
    half = own // 2
    share = half // PARTS
    top = cz - 1
    me_e, me_s = lax.axis_index("ens"), lax.axis_index("space")
    scale = math.sqrt(members - 1.0)
    lo_side, hi_side = me_s > 0, me_s < n_s - 1

    def local(src, dst, i):
        copy = pltpu.make_async_copy(src, dst, load.at[i])
        copy.start()
        return copy

    quarter = own // 4
    loads = []
    for i in range(4):
        at = pl.ds(i * quarter, quarter)
        loads.append(local(u_hbm.at[at], u_ref.at[at], 2 * i))
        loads.append(local(k_hbm.at[at], k_ref.at[at], 2 * i + 1))
    small = [
        local(slots_hbm, slots_ref, 8),
        local(noise_hbm, noise_ref, 9),
        local(values_hbm, values_ref, 10),
        local(std_hbm, std_ref, 11),
        local(params_hbm, all_params.at[me_e], 12),
    ]

    def ens_peer(d):
        return (lax.rem(me_e + d, n_e), me_s)

    def space_peer(d):
        return (me_e, lax.rem(me_s + d, n_s))

    barrier = pltpu.get_barrier_semaphore()
    for d in range(1, n_e):
        pl.semaphore_signal(barrier, inc=1, device_id=ens_peer(d), device_id_type=MESH)

    def at_distance(d, what):
        for there, peer in ((me_s >= d, me_s - d), (me_s + d < n_s, me_s + d)):
            @pl.when(there)
            def _():
                what((me_e, peer))

    def signal(sem, peer):
        pl.semaphore_signal(sem, inc=1, device_id=peer, device_id_type=MESH)

    at_distance(1, functools.partial(signal, barrier))
    pad_rows(fu, fk)
    def peers_at(d):
        return (me_s >= d).astype(jnp.int32) + (me_s + d < n_s).astype(jnp.int32)

    pl.semaphore_wait(barrier, n_e - 1 + peers_at(1))

    def gate_signal(r):
        at_distance(1 << r, functools.partial(signal, gate.at[r]))

    def gate_wait(r):
        pl.semaphore_wait(gate.at[r], peers_at(1 << r))

    rounds = gate.shape[0]
    gate_signal(0)

    def remote(src, dst, ssem, rsem, peer):
        return pltpu.make_async_remote_copy(
            src_ref=src, dst_ref=dst, send_sem=ssem, recv_sem=rsem,
            device_id=peer, device_id_type=MESH,
        )

    def send(*args):
        copy = remote(*args)
        copy.start()
        return copy

    above, under = (me_e, lax.rem(me_s + 1, n_s)), (me_e, lax.rem(me_s + n_s - 1, n_s))

    def on_sides(sides, pair, what):
        for side, copies in zip(sides, pair):
            @pl.when(side)
            def _():
                for copy in copies:
                    getattr(copy, what)()

    def start_pair(pair):
        on_sides((hi_side, lo_side), pair, "start")

    def wait_send_pair(pair):
        on_sides((hi_side, lo_side), pair, "wait_send")

    def wait_recv_pair(pair):
        on_sides((lo_side, hi_side), pair, "wait_recv")

    ask = (
        [remote(slots_hbm, asked.at[0], send_q.at[0], recv_q.at[0], above)],
        [remote(slots_hbm, asked.at[1], send_q.at[1], recv_q.at[1], under)],
    )
    start_pair(ask)

    def bulk(i):
        at, src_up, src_down = (
            pl.ds(i * share, share), pl.ds(i * share, share), pl.ds(half + i * share, share)
        )
        s, r = send_b.at[i], recv_b.at[i]
        return (
            [
                remote(u_hbm.at[src_up, top], ulo.at[at], s.at[0], r.at[0], above),
                remote(k_hbm.at[src_up, top], klo.at[at], s.at[1], r.at[1], above),
            ],
            [
                remote(u_hbm.at[src_down, 0], uhi.at[at], s.at[2], r.at[2], under),
                remote(k_hbm.at[src_down, 0], khi.at[at], s.at[3], r.at[3], under),
            ],
        )

    def returned(i):
        at = pl.ds(i * share, share)
        s, r = send_r.at[i], recv_r.at[i]
        return (
            [remote(back.at[1, at], ret.at[0, at], s.at[0], r.at[0], above)],
            [remote(back.at[0, at], ret.at[1, at], s.at[1], r.at[1], under)],
        )

    bulks = [bulk(i) for i in range(PARTS)]
    returns = [returned(i) for i in range(PARTS)]

    def border(i):
        wait_recv_pair(bulks[i])

        def one(m, carry):
            for e, z, shift, un_ref, kn_ref, side in (
                (0, 0, 0, ulo, klo, lo_side), (1, top, half, uhi, khi, hi_side),
            ):
                un = jnp.where(side, un_ref[m].astype(f32), 0.0)
                kn = jnp.where(side, kn_ref[m].astype(f32), 0.0)
                u, k = u_ref[m + shift, z].astype(f32), k_ref[m + shift, z].astype(f32)
                value = half_step * (k + kn) * (un - u)
                flux[e, m] = value
                back[e, m] = squeeze(value)
            return carry

        lax.fori_loop(i * share, (i + 1) * share, one, 0)

    for i in range(EARLY):
        start_pair(bulks[i])
    params_copies = [
        send(params_hbm, all_params.at[me_e], send_p.at[d], recv_p.at[d], ens_peer(d))
        for d in range(1, n_e)
    ]

    def quarter_stencil(i):
        stencil(i * quarter, (i + 1) * quarter, u_ref, k_ref, pred, fu, fk, fy)

    for i in range(BEFORE):
        for copy in loads[2 * i : 2 * i + 2]:
            copy.wait()
        quarter_stencil(i)
    for copy in loads[2 * BEFORE :] + small:
        copy.wait()
    gate_wait(0)

    lane_row = lax.broadcasted_iota(jnp.int32, (ny, WIDE), 0)
    deep_row = lax.broadcasted_iota(jnp.int32, (2 * ny, WIDE), 0)
    x_row = lax.broadcasted_iota(jnp.int32, (nx, WIDE), 0)
    bits_y, bits_x = int(math.log2(ny)), int(math.log2(nx))

    def coordinates(p):
        y = p & (ny - 1)
        x = lax.shift_right_logical(p, bits_y) & (nx - 1)
        return y, x, lax.shift_right_logical(p, bits_y + bits_x)

    def columns(c):
        return pl.ds(pl.multiple_of(c * WIDE, WIDE), WIDE)

    def pick(layer, hot, mask):
        g = jnp.dot(layer, hot, preferred_element_type=f32)
        return jnp.sum(jnp.where(mask, g.reshape(own, nx, WIDE), 0.0), axis=1)

    reply = (
        [remote(answer.at[1], got.at[0], send_w.at[0], recv_w.at[0], above)],
        [remote(answer.at[0], got.at[1], send_w.at[1], recv_w.at[1], under)],
    )
    wait_recv_pair(ask)
    for e, z in ((1, top), (0, 0)):
        def answer_chunk(c, carry):
            at = columns(c)
            y, x, _ = coordinates(asked[e, :, at])
            hot = jnp.where(lane_row == y, 1.0, 0.0).astype(bf16)
            mask = (x_row == x)[None]
            for f, ref in enumerate((u_ref, k_ref)):
                layer = ref[:, z].reshape(own * nx, ny)
                answer[e, f, :, at] = pick(layer, hot, mask).astype(bf16)
            return carry

        lax.fori_loop(0, chunks, answer_chunk, 0)

        @pl.when((lo_side, hi_side)[e])
        def _():
            reply[1 - e][0].start()

    for i in range(EARLY, LATE):
        start_pair(bulks[i])
    for r in range(1, rounds):
        gate_signal(r)
        if r < rounds - 1:
            gate_wait(r)
    for i in range(BEFORE, 4):
        quarter_stencil(i)
    border(0)
    for i in range(FIRST):
        start_pair(returns[i])

    lane = lax.broadcasted_iota(jnp.int32, (own, ny), 1)
    rows = pred.shape[1]
    flat = pred.reshape(own * rows, ny)
    pair = me_e + 1 - 2 * lax.rem(me_e, 2)
    partner = (pair, me_s)
    hops = n_e // 2

    def hand(d, c):
        block = all_picked.at[lax.rem(me_e + n_e - 2 * d, n_e), c]
        src = picked.at[c] if d == 0 else block
        return remote(src, block, send_h.at[d, c], recv_h.at[d, c], partner)

    def across(d, c):
        dst = all_picked.at[me_e, c]
        return remote(picked.at[c], dst, send_a.at[d, c], recv_a.at[d, c], ens_peer(2 * d))

    def relay(c):
        for d in range(1, hops):
            across(d, c).wait_recv()
            hand(d, c).start()

    def reading(c):
        y, x, z = coordinates(slots_ref[:, columns(c)])
        spot = jnp.where(z == 0, y, jnp.where(z == top, y + ny, -1))
        hot = jnp.where(deep_row == spot, 1.0, 0.0).astype(bf16)
        mask = (x_row == x)[None]
        for f, ref in enumerate((u_ref, k_ref)):
            layer = jnp.concatenate([ref[:, 0], ref[:, top]], axis=2)
            own_at[f, c] = pick(layer.reshape(own * nx, 2 * ny), hot, mask)
        for h in range(0, WIDE, ny):
            def step(s, acc):
                for i in range(unroll):
                    jj = s * unroll + i
                    p = pos_ref[c * WIDE + h + jj]
                    v = flat[pl.ds(lax.shift_right_logical(p, bits_y), own, stride=rows), :]
                    v = pltpu.roll(v, (jj - p) & (ny - 1), 1)
                    acc = jnp.where(lane == jj, v, acc)
                return acc

            unroll = ny // 2
            acc = lax.fori_loop(0, ny // unroll, step, jnp.zeros((own, ny), f32))
            picked[c, :, h : h + ny] = acc

    def complete(c):
        at = columns(c)
        _, _, z = coordinates(slots_ref[:, at])
        u_at, k_at = own_at[0, c], own_at[1, c]
        value = picked[c]
        for e, here, side in ((0, z == 0, lo_side), (1, z == top, hi_side)):
            other = jnp.logical_and(here, side)
            u_n = jnp.where(other, got[e, 0, :, at].astype(f32), 0.0)
            k_n = jnp.where(other, got[e, 1, :, at].astype(f32), 0.0)
            value += jnp.where(here, half_step * (k_at + k_n) * (u_n - u_at), 0.0)
        picked[c] = value
        all_picked[me_e, c] = value
        hand(0, c).start()
        for d in range(1, hops):
            across(d, c).start()

    ahead = min(AHEAD, chunks)

    def first_readings(c, carry):
        reading(c)
        return carry

    lax.fori_loop(0, ahead, first_readings, 0)
    wait_recv_pair(reply)

    def more_readings(c, carry):
        reading(c + ahead)
        complete(c)

        @pl.when(c > 0)
        def _():
            relay(c - 1)

        return carry

    lax.fori_loop(0, chunks - ahead, more_readings, 0)
    def last_readings(c, carry):
        complete(c)

        @pl.when(c > 0)
        def _():
            relay(c - 1)

        return carry

    lax.fori_loop(chunks - ahead, chunks, last_readings, 0)
    relay(chunks - 1)

    part[...] = jnp.zeros_like(part)

    def product(c, carry):
        at = columns(c)
        for d in range(hops):
            hand(d, c).wait_recv()
        mine = picked[c]
        live = lax.broadcasted_iota(jnp.int32, (1, WIDE), 1) + c * WIDE < count_ref[0]
        std = std_ref[:, at]
        inverse = jnp.where(live, 1.0 / (std * scale), 0.0)
        misfit = jnp.where(live, (values_ref[:, at] - mine) / std + noise_ref[:, at], 0.0)
        everyone = all_picked[:, c].reshape(members, WIDE)
        centre = jnp.sum(everyone, axis=0, keepdims=True) / members
        spread = (everyone - centre) * inverse
        left = jnp.concatenate([spread, misfit], axis=0)
        part[...] += lax.dot_general(
            left, spread, (((1,), (1,)), ((), ())),
            precision=HI, preferred_element_type=f32,
        )
        return carry

    lax.fori_loop(0, chunks, product, 0)
    grams, crosses = members // n_s, own // n_s
    pieces[:, :grams] = part[:members].reshape(n_s, grams, members)
    for i in range(n_s):
        pieces[i, grams : grams + crosses] = part[members + i * crosses : members + (i + 1) * crosses]
    gate_wait(rounds - 1)
    scatter = []
    for d in range(1, n_s):
        src = pieces.at[lax.rem(me_s + d, n_s)]
        scatter.append(send(src, parts.at[d], send_s.at[d], recv_s.at[d], space_peer(d)))
    for i in range(LATE, PARTS):
        start_pair(bulks[i])
    for i in range(1, LATE):
        border(i)
    for i in range(FIRST, FIRST + MIDDLE):
        start_pair(returns[i])
    acc = pieces[me_s]
    for d in range(1, n_s):
        scatter[d - 1].wait()
        acc += parts[d]
    total[...] = acc
    sums[me_s] = acc
    gather = [
        send(total, sums.at[me_s], send_g.at[d], recv_g.at[d], space_peer(d))
        for d in range(1, n_s)
    ]
    for i in range(FIRST + MIDDLE, LATE):
        start_pair(returns[i])
    for i in range(LATE, PARTS):
        border(i)
        start_pair(returns[i])

    def add_flux(m, carry):
        bottom, upper = pl.ds(0, nx), pl.ds(top * nx, nx)
        pred[m, bottom] = pred[m, bottom] + flux[0, m]
        pred[m + half, upper] = pred[m + half, upper] + flux[1, m]
        return carry

    lax.fori_loop(0, half, add_flux, 0)
    for copy in gather:
        copy.wait()
    gram = sums[:, :grams].reshape(members, members)
    cross = jnp.concatenate([sums[i, grams : grams + crosses] for i in range(n_s)], axis=0)
    for copy in params_copies:
        copy.wait()
    weights = solve(gram, cross, work)
    everyones = all_params[...].reshape(members, -1)
    centre = jnp.sum(everyones, axis=0, keepdims=True) / members
    anomaly = (everyones - centre) / math.sqrt(members - 1.0)
    posterior_ref[...] = all_params[me_e] + jnp.dot(
        weights, anomaly, precision=HI, preferred_element_type=f32
    )

    def add_returned(m, carry):
        for e, z, shift, side in ((0, 0, half, lo_side), (1, top, 0, hi_side)):
            at = pl.ds(z * nx, nx)
            u, k = u_ref[m + shift, z].astype(f32), k_ref[m + shift, z].astype(f32)
            lost = jnp.where(side, expand(ret[e, m]), half_step * k * u)
            pred[m + shift, at] = pred[m + shift, at] - lost
        return carry

    for i in range(PARTS):
        wait_recv_pair(returns[i])
        lax.fori_loop(i * share, (i + 1) * share, add_returned, 0)

    for pair in [ask, reply] + bulks + returns:
        wait_send_pair(pair)

    def drain(c, carry):
        for d in range(hops):
            hand(d, c).wait_send()
        for d in range(1, hops):
            across(d, c).wait_send()
        return carry

    lax.fori_loop(0, chunks, drain, 0)


def analysis(n_e, n_s, position, count, noise, values, std, params, u, k):
    own, cz, nx, ny = u.shape
    slots = position.shape[0]
    chunks = slots // WIDE
    members = own * n_e
    half = own // 2
    piece = members // n_s + 8 * pl.cdiv(own // n_s, 8)
    vmem = pl.BlockSpec(memory_space=pltpu.VMEM)
    smem = pl.BlockSpec(memory_space=pltpu.SMEM)
    hbm = pl.BlockSpec(memory_space=pltpu.HBM)
    dma = pltpu.SemaphoreType.DMA
    field = (own, cz * nx + PAD, ny)
    layers = pltpu.VMEM((half, nx, ny), u.dtype)
    group = 4
    return pl.pallas_call(
        functools.partial(analysis_kernel, n_e, n_s),
        in_specs=[smem, smem] + [hbm] * 7,
        out_specs=[vmem, vmem],
        out_shape=[pltpu.VMEM(field, f32), pltpu.VMEM(params.shape, f32)],
        scratch_shapes=[
            pltpu.VMEM(u.shape, u.dtype),
            pltpu.VMEM(k.shape, k.dtype),
            pltpu.VMEM((group, cz, nx + 2 * PAD, ny), f32),
            pltpu.VMEM((group, cz, nx + 2 * PAD, ny), f32),
            pltpu.VMEM((group, cz * nx, ny), f32),
            layers, layers, layers, layers,
            pltpu.VMEM((2, half, nx, ny), f32),
            pltpu.VMEM((2, half, nx, ny), bf16),
            pltpu.VMEM((2, half, nx, ny), bf16),
            pltpu.VMEM((1, slots), jnp.int32),
            pltpu.VMEM((own, slots), f32),
            pltpu.VMEM((1, slots), f32),
            pltpu.VMEM((1, slots), f32),
            pltpu.VMEM((2, 1, slots), jnp.int32),
            pltpu.VMEM((2, 2, own, slots), bf16),
            pltpu.VMEM((2, 2, own, slots), bf16),
            pltpu.VMEM((chunks, own, WIDE), f32),
            pltpu.VMEM((n_e, chunks, own, WIDE), f32),
            pltpu.VMEM((n_e,) + params.shape, f32),
            pltpu.VMEM((2, chunks, own, WIDE), f32),
            pltpu.VMEM((members + own, members), f32),
            pltpu.VMEM((n_s, piece, members), f32),
            pltpu.VMEM((n_s, piece, members), f32),
            pltpu.VMEM((piece, members), f32),
            pltpu.VMEM((n_s, piece, members), f32),
            pltpu.VMEM((members + own, members), f32),
            pltpu.SemaphoreType.REGULAR((max(1, (n_s - 1).bit_length()),)),
            dma((13,)),
        ]
        + [dma((2,))] * 4
        + [dma((PARTS, 4))] * 2
        + [dma((PARTS, 2))] * 2
        + [dma((n_e // 2, chunks))] * 4
        + [dma((n_e,))] * 2
        + [dma((n_s,))] * 4,
        compiler_params=pltpu.CompilerParams(
            collective_id=0,
            has_side_effects=True,
            vmem_limit_bytes=VMEM_BYTES - 4 * math.prod(field) - (512 << 10),
        ),
        name="analysis",
    )(
        position, count, position.reshape(1, -1), noise, values.reshape(1, -1),
        std.reshape(1, -1), params, u, k,
    )


def finish_kernel(pred_ref, post_ref, o_ref, posterior_ref, sem):
    members, cz, nx, ny = o_ref.shape
    block = members // sem.shape[0]
    copies = []
    for i in range(sem.shape[0]):
        for z in range(cz):
            at = pl.ds(i * block, block)
            src = pred_ref.at[at, pl.ds(z * nx, nx)]
            copies.append(pltpu.make_async_copy(src, o_ref.at[at, z], sem.at[i, z]))
    for copy in copies:
        copy.start()
    posterior_ref[...] = post_ref[...]
    for copy in copies:
        copy.wait()


def finish(shape, pred, posterior):
    vmem = pl.BlockSpec(memory_space=pltpu.VMEM)
    return pl.pallas_call(
        finish_kernel,
        in_specs=[vmem, vmem],
        out_specs=[pl.BlockSpec(memory_space=pl.ANY), vmem],
        out_shape=[
            jax.ShapeDtypeStruct(shape, jnp.float32),
            jax.ShapeDtypeStruct(posterior.shape, jnp.float32),
        ],
        scratch_shapes=[pltpu.SemaphoreType.DMA((4, shape[1]))],
        compiler_params=pltpu.CompilerParams(vmem_limit_bytes=20 << 20),
        name="finish",
    )(pred, posterior)


def shards(n_e, n_s, u, k, position, count, values, std, noise, params):
    pred, posterior = analysis(n_e, n_s, position, count, noise, values, std, params, u, k)
    pred, posterior = finish(u.shape, pred, posterior)
    return posterior, pred


def solution(mesh):
    in_specs = (
        P("ens", "space", None, None),
        P("ens", "space", None, None),
        P("space"),
        P("space"),
        P("space"),
        P("space"),
        P("ens", "space"),
        P("ens", "space"),
    )
    out_specs = (P("ens", "space"), P("ens", "space", None, None))
    body = functools.partial(shards, mesh.shape["ens"], mesh.shape["space"])
    return jax.shard_map(body, mesh=mesh, in_specs=in_specs, out_specs=out_specs, check_vma=False)
```

```python
import functools
import math

import jax
import jax.numpy as jnp
from jax import lax
from jax.experimental import pallas as pl
from jax.experimental.pallas import tpu as pltpu
from jax.sharding import PartitionSpec as P

half_step = 0.04
HI = lax.Precision.HIGHEST
MESH = pl.DeviceIdType.MESH
VMEM_BYTES = 67043328
PARTS = 8
EARLY = 1
LATE = 6
FIRST = 1
BEFORE = 2
AHEAD = 3
MIDDLE = 0
ADDED = 4
BACK = 1
PAD = 8
WIDE = 256
f32 = jnp.float32
bf16 = jnp.bfloat16


def squeeze(f):
    p = f * f
    p = p * p
    p = p * p
    return jnp.where(f < 0.0, -p, p).astype(bf16)


def expand(y):
    y = y.astype(f32)
    quarter = lax.rsqrt(lax.rsqrt(jnp.abs(y)))
    root = jnp.where(y == 0.0, 0.0, quarter * lax.rsqrt(quarter))
    return jnp.where(y < 0.0, -root, root)


def pad_rows(fu, fk):
    nx = fu.shape[2] - 2 * PAD
    for f in (fu, fk):
        zero = jnp.zeros(f.shape[:2] + (PAD, f.shape[3]), f32)
        f[:, :, :PAD] = zero
        f[:, :, PAD + nx :] = zero


def stencil(lo, hi, u_ref, k_ref, o_ref, fu, fk, fy):
    cz, nx, ny = u_ref.shape[1:]
    group = fu.shape[0]
    r = lax.broadcasted_iota(jnp.int32, (ny, ny), 0)
    c = lax.broadcasted_iota(jnp.int32, (ny, ny), 1)
    eye, following, previous = r == c, r == c + 1, r + 1 == c
    one = lambda mask: jnp.where(mask, 1.0, 0.0)
    plus = [one(following) + one(eye), one(previous) + one(eye)]
    minus = [one(following) - one(eye), one(previous) - one(eye)]
    plus = jnp.concatenate(plus, axis=1).astype(bf16)
    minus = jnp.concatenate(minus, axis=1).astype(bf16)
    span = 32

    def members(i, carry):
        first = lo + i * group
        for w in range(group):
            ks = k_ref[first + w].reshape(cz * nx, ny)
            us = u_ref[first + w].reshape(cz * nx, ny)
            flux = jnp.dot(ks, plus, preferred_element_type=f32) * jnp.dot(
                us, minus, preferred_element_type=f32
            )
            fy[w] = flux[:, :ny] + flux[:, ny:]
            for z in range(cz):
                fu[w, z, PAD : PAD + nx] = u_ref[first + w, z].astype(f32)
                fk[w, z, PAD : PAD + nx] = k_ref[first + w, z].astype(f32)
        for w in range(group):
            for x in range(0, nx, span):
                at = slice(PAD + x, PAD + x + span)
                after = slice(PAD + x + 1, PAD + x + span + 1)
                before = slice(PAD + x - 1, PAD + x + span - 1)
                below = None
                u, k = fu[w, 0, at], fk[w, 0, at]
                for z in range(cz):
                    total = (k + fk[w, z, after]) * (fu[w, z, after] - u)
                    total += (k + fk[w, z, before]) * (fu[w, z, before] - u)
                    total += fy[w, z * nx + x : z * nx + x + span]
                    if below is not None:
                        total -= below
                    if z < cz - 1:
                        u_next, k_next = fu[w, z + 1, at], fk[w, z + 1, at]
                        below = (k + k_next) * (u_next - u)
                        total += below
                    o_ref[first + w, z * nx + x : z * nx + x + span] = u + half_step * total
                    if z < cz - 1:
                        u, k = u_next, k_next
        return carry

    lax.fori_loop(0, (hi - lo) // group, members, 0)


def solve(gram, cross, work):
    members = gram.shape[1]
    rows = lax.broadcasted_iota(jnp.int32, (members, members), 0)
    cols = lax.broadcasted_iota(jnp.int32, (members, members), 1)
    lane = lax.broadcasted_iota(jnp.int32, (1, members), 1)
    work[:members] = gram + jnp.where(rows == cols, 1.0, 0.0)
    work[members:] = cross

    pivots = 8
    segments = 4
    span = members // segments

    def step(lo, s, carry):
        first = lo + s * pivots
        t = work[lo:]
        here = [lane == first + i for i in range(pivots)]
        columns = [
            jnp.sum(jnp.where(here[i], t, 0.0), axis=1, keepdims=True) for i in range(pivots)
        ]
        rows = [work[pl.ds(first + i, 1), :] for i in range(pivots)]
        corner = [
            [jnp.sum(jnp.where(here[j], rows[i], 0.0), axis=1, keepdims=True) for j in range(pivots)]
            for i in range(pivots)
        ]
        rows = [rows[i] - jnp.where(here[i], 1.0, 0.0) for i in range(pivots)]
        for i in range(pivots):
            inverse = 1.0 / corner[i][i]
            rows[i] = rows[i] * inverse
            for j in range(i + 1, pivots):
                corner[i][j] = corner[i][j] * inverse
            for l in range(i + 1, pivots):
                rows[l] = rows[l] - corner[l][i] * rows[i]
                for j in range(i + 1, pivots):
                    corner[l][j] = corner[l][j] - corner[l][i] * corner[i][j]
        for i in range(pivots - 1, -1, -1):
            for j in range(i + 1, pivots):
                rows[i] = rows[i] - corner[i][j] * rows[j]
        for i in range(pivots):
            t = t - columns[i] * rows[i]
        work[lo:] = t
        return carry

    for part in range(segments):
        lax.fori_loop(0, span // pivots, functools.partial(step, part * span), 0)
    return work[members:]


def analysis_kernel(
    n_e, n_s, pos_hbm, count_hbm, slots_hbm, noise_hbm, values_hbm, std_hbm, params_hbm,
    u_hbm, k_hbm,
    pred, posterior_ref,
    u_ref, k_ref, fu, fk, fy, ulo, klo, uhi, khi, flux, back, ret,
    pos_ref, count_ref, slots_ref, noise_ref, values_ref, std_ref, asked, answer, got, picked, all_picked,
    all_params, own_at, part, pieces, parts, total, sums, work, anomaly,
    gate, load, send_q, recv_q, send_w, recv_w, send_b, recv_b, send_r, recv_r,
    send_a, recv_a, send_h, recv_h, send_p, recv_p, send_s, recv_s, send_g, recv_g,
):
    own, cz, nx, ny = u_ref.shape
    slots = slots_ref.shape[1]
    chunks = slots // WIDE
    members = own * n_e
    half = own // 2
    share = half // PARTS
    top = cz - 1
    me_e, me_s = lax.axis_index("ens"), lax.axis_index("space")
    scale = math.sqrt(members - 1.0)
    lo_side, hi_side = me_s > 0, me_s < n_s - 1

    def local(src, dst, i):
        copy = pltpu.make_async_copy(src, dst, load.at[i])
        copy.start()
        return copy

    quarter = own // 4
    loads = []
    for i in range(4):
        at = pl.ds(i * quarter, quarter)
        loads.append(local(u_hbm.at[at], u_ref.at[at], 2 * i))
        loads.append(local(k_hbm.at[at], k_ref.at[at], 2 * i + 1))
    small = [
        local(slots_hbm, slots_ref, 8),
        local(pos_hbm, pos_ref, 13),
        local(count_hbm, count_ref, 14),
        local(noise_hbm, noise_ref, 9),
        local(values_hbm, values_ref, 10),
        local(std_hbm, std_ref, 11),
        local(params_hbm, all_params.at[me_e], 12),
    ]

    def ens_peer(d):
        return (lax.rem(me_e + d, n_e), me_s)

    def space_peer(d):
        return (me_e, lax.rem(me_s + d, n_s))

    barrier = pltpu.get_barrier_semaphore()
    for d in range(1, n_e):
        pl.semaphore_signal(barrier, inc=1, device_id=ens_peer(d), device_id_type=MESH)

    def at_distance(d, what):
        for there, peer in ((me_s >= d, me_s - d), (me_s + d < n_s, me_s + d)):
            @pl.when(there)
            def _():
                what((me_e, peer))

    def signal(sem, peer):
        pl.semaphore_signal(sem, inc=1, device_id=peer, device_id_type=MESH)

    at_distance(1, functools.partial(signal, barrier))
    pad_rows(fu, fk)
    def peers_at(d):
        return (me_s >= d).astype(jnp.int32) + (me_s + d < n_s).astype(jnp.int32)

    pl.semaphore_wait(barrier, n_e - 1 + peers_at(1))

    def gate_signal(r):
        at_distance(1 << r, functools.partial(signal, gate.at[r]))

    def gate_wait(r):
        pl.semaphore_wait(gate.at[r], peers_at(1 << r))

    rounds = gate.shape[0]
    gate_signal(0)

    def remote(src, dst, ssem, rsem, peer):
        return pltpu.make_async_remote_copy(
            src_ref=src, dst_ref=dst, send_sem=ssem, recv_sem=rsem,
            device_id=peer, device_id_type=MESH,
        )

    def send(*args):
        copy = remote(*args)
        copy.start()
        return copy

    above, under = (me_e, lax.rem(me_s + 1, n_s)), (me_e, lax.rem(me_s + n_s - 1, n_s))

    def on_sides(sides, pair, what):
        for side, copies in zip(sides, pair):
            @pl.when(side)
            def _():
                for copy in copies:
                    getattr(copy, what)()

    def start_pair(pair):
        on_sides((hi_side, lo_side), pair, "start")

    def wait_send_pair(pair):
        on_sides((hi_side, lo_side), pair, "wait_send")

    def wait_recv_pair(pair):
        on_sides((lo_side, hi_side), pair, "wait_recv")

    ask = (
        [remote(slots_hbm, asked.at[0], send_q.at[0], recv_q.at[0], above)],
        [remote(slots_hbm, asked.at[1], send_q.at[1], recv_q.at[1], under)],
    )
    start_pair(ask)

    def bulk(i):
        at, src_up, src_down = (
            pl.ds(i * share, share), pl.ds(i * share, share), pl.ds(half + i * share, share)
        )
        s, r = send_b.at[i], recv_b.at[i]
        return (
            [
                remote(u_hbm.at[src_up, top], ulo.at[at], s.at[0], r.at[0], above),
                remote(k_hbm.at[src_up, top], klo.at[at], s.at[1], r.at[1], above),
            ],
            [
                remote(u_hbm.at[src_down, 0], uhi.at[at], s.at[2], r.at[2], under),
                remote(k_hbm.at[src_down, 0], khi.at[at], s.at[3], r.at[3], under),
            ],
        )

    def returned(i):
        at = pl.ds(i * share, share)
        s, r = send_r.at[i], recv_r.at[i]
        return (
            [remote(back.at[1, at], ret.at[0, at], s.at[0], r.at[0], above)],
            [remote(back.at[0, at], ret.at[1, at], s.at[1], r.at[1], under)],
        )

    bulks = [bulk(i) for i in range(PARTS)]
    returns = [returned(i) for i in range(PARTS)]

    def border(i):
        wait_recv_pair(bulks[i])

        def one(m, carry):
            for e, z, shift, un_ref, kn_ref, side in (
                (0, 0, 0, ulo, klo, lo_side), (1, top, half, uhi, khi, hi_side),
            ):
                un = jnp.where(side, un_ref[m].astype(f32), 0.0)
                kn = jnp.where(side, kn_ref[m].astype(f32), 0.0)
                u, k = u_ref[m + shift, z].astype(f32), k_ref[m + shift, z].astype(f32)
                value = half_step * (k + kn) * (un - u)
                flux[e, m] = value
                back[e, m] = squeeze(value)
            return carry

        lax.fori_loop(i * share, (i + 1) * share, one, 0)

    for i in range(EARLY):
        start_pair(bulks[i])
    params_copies = [
        send(params_hbm, all_params.at[me_e], send_p.at[d], recv_p.at[d], ens_peer(d))
        for d in range(1, n_e)
    ]

    def quarter_stencil(i):
        stencil(i * quarter, (i + 1) * quarter, u_ref, k_ref, pred, fu, fk, fy)

    for i in range(BEFORE):
        for copy in loads[2 * i : 2 * i + 2]:
            copy.wait()
        quarter_stencil(i)
    for copy in loads[2 * BEFORE :] + small:
        copy.wait()
    gate_wait(0)

    deep_row = lax.broadcasted_iota(jnp.int32, (2 * ny, WIDE), 0)
    x_row = lax.broadcasted_iota(jnp.int32, (nx, WIDE), 0)
    bits_y, bits_x = int(math.log2(ny)), int(math.log2(nx))

    def coordinates(p):
        y = p & (ny - 1)
        x = lax.shift_right_logical(p, bits_y) & (nx - 1)
        return y, x, lax.shift_right_logical(p, bits_y + bits_x)

    def columns(c):
        return pl.ds(pl.multiple_of(c * WIDE, WIDE), WIDE)

    def pick(layer, hot, mask):
        lines = layer.shape[1]
        g = jnp.dot(layer.reshape(own * lines, 2 * ny), hot, preferred_element_type=f32)
        return jnp.sum(jnp.where(mask, g.reshape(own, lines, WIDE), 0.0), axis=1)

    reply = (
        [remote(answer.at[1], got.at[0], send_w.at[0], recv_w.at[0], above)],
        [remote(answer.at[0], got.at[1], send_w.at[1], recv_w.at[1], under)],
    )
    wait_recv_pair(ask)
    for e, z in ((1, top), (0, 0)):
        def answer_chunk(c, carry):
            at = columns(c)
            y, x, _ = coordinates(asked[e, :, at])
            spot = jnp.where(x < nx // 2, y, y + ny)
            hot = jnp.where(deep_row == spot, 1.0, 0.0).astype(bf16)
            mask = (x_row[: nx // 2] == (x & (nx // 2 - 1)))[None]
            for f, ref in enumerate((u_ref, k_ref)):
                layer = jnp.concatenate([ref[:, z, : nx // 2], ref[:, z, nx // 2 :]], axis=2)
                answer[e, f, :, at] = pick(layer, hot, mask).astype(bf16)
            return carry

        lax.fori_loop(0, chunks, answer_chunk, 0)

        @pl.when((lo_side, hi_side)[e])
        def _():
            reply[1 - e][0].start()

    for i in range(EARLY, LATE):
        start_pair(bulks[i])
    for r in range(1, rounds):
        gate_signal(r)
        if r < rounds - 1:
            gate_wait(r)
    for i in range(BEFORE, 4):
        quarter_stencil(i)
    for i in range(FIRST):
        border(i)
        start_pair(returns[i])

    lane = lax.broadcasted_iota(jnp.int32, (own, ny), 1)
    rows = pred.shape[1]
    flat = pred.reshape(own * rows, ny)
    pair = me_e + 1 - 2 * lax.rem(me_e, 2)
    partner = (pair, me_s)
    hops = n_e // 2

    def hand(d, c):
        block = all_picked.at[lax.rem(me_e + n_e - 2 * d, n_e), c]
        src = picked.at[c] if d == 0 else block
        return remote(src, block, send_h.at[d, c], recv_h.at[d, c], partner)

    def across(d, c):
        dst = all_picked.at[me_e, c]
        return remote(picked.at[c], dst, send_a.at[d, c], recv_a.at[d, c], ens_peer(2 * d))

    def relay(c):
        for d in range(1, hops):
            across(d, c).wait_recv()
            hand(d, c).start()

    def reading(c):
        y, x, z = coordinates(slots_ref[:, columns(c)])
        spot = jnp.where(z == 0, y, jnp.where(z == top, y + ny, -1))
        hot = jnp.where(deep_row == spot, 1.0, 0.0).astype(bf16)
        mask = (x_row == x)[None]
        for f, ref in enumerate((u_ref, k_ref)):
            layer = jnp.concatenate([ref[:, 0], ref[:, top]], axis=2)
            own_at[f, c] = pick(layer, hot, mask)
        for h in range(0, WIDE, ny):
            def step(s, acc):
                for i in range(unroll):
                    jj = s * unroll + i
                    p = pos_ref[c * WIDE + h + jj]
                    v = flat[pl.ds(lax.shift_right_logical(p, bits_y), own, stride=rows), :]
                    v = pltpu.roll(v, (jj - p) & (ny - 1), 1)
                    acc = jnp.where(lane == jj, v, acc)
                return acc

            unroll = ny // 2
            acc = lax.fori_loop(0, ny // unroll, step, jnp.zeros((own, ny), f32))
            picked[c, :, h : h + ny] = acc

    def complete(c):
        at = columns(c)
        _, _, z = coordinates(slots_ref[:, at])
        u_at, k_at = own_at[0, c], own_at[1, c]
        value = picked[c]
        for e, here, side in ((0, z == 0, lo_side), (1, z == top, hi_side)):
            other = jnp.logical_and(here, side)
            u_n = jnp.where(other, got[e, 0, :, at].astype(f32), 0.0)
            k_n = jnp.where(other, got[e, 1, :, at].astype(f32), 0.0)
            value += jnp.where(here, half_step * (k_at + k_n) * (u_n - u_at), 0.0)
        picked[c] = value
        all_picked[me_e, c] = value
        hand(0, c).start()
        for d in range(1, hops):
            across(d, c).start()

    ahead = min(AHEAD, chunks)

    def first_readings(c, carry):
        reading(c)
        return carry

    lax.fori_loop(0, ahead, first_readings, 0)
    wait_recv_pair(reply)

    def more_readings(c, carry):
        reading(c + ahead)
        complete(c)

        @pl.when(c > 0)
        def _():
            relay(c - 1)

        return carry

    lax.fori_loop(0, chunks - ahead, more_readings, 0)
    def last_readings(c, carry):
        complete(c)

        @pl.when(c > 0)
        def _():
            relay(c - 1)

        return carry

    lax.fori_loop(chunks - ahead, chunks, last_readings, 0)
    relay(chunks - 1)

    part[...] = jnp.zeros_like(part)

    def product(c, carry):
        at = columns(c)
        for d in range(hops):
            hand(d, c).wait_recv()
        mine = picked[c]
        live = lax.broadcasted_iota(jnp.int32, (1, WIDE), 1) + c * WIDE < count_ref[...]
        std = std_ref[:, at]
        inverse = jnp.where(live, 1.0 / (std * scale), 0.0)
        misfit = jnp.where(live, (values_ref[:, at] - mine) / std + noise_ref[:, at], 0.0)
        everyone = all_picked[:, c].reshape(members, WIDE)
        centre = jnp.sum(everyone, axis=0, keepdims=True) / members
        spread = (everyone - centre) * inverse
        left = jnp.concatenate([spread, misfit], axis=0)
        part[...] += lax.dot_general(
            left, spread, (((1,), (1,)), ((), ())),
            precision=HI, preferred_element_type=f32,
        )
        return carry

    lax.fori_loop(0, chunks, product, 0)
    grams, crosses = members // n_s, own // n_s
    pieces[:, :grams] = part[:members].reshape(n_s, grams, members)
    for i in range(n_s):
        pieces[i, grams : grams + crosses] = part[members + i * crosses : members + (i + 1) * crosses]
    def add_flux(m, carry):
        bottom, upper = pl.ds(0, nx), pl.ds(top * nx, nx)
        pred[m, bottom] = pred[m, bottom] + flux[0, m]
        pred[m + half, upper] = pred[m + half, upper] + flux[1, m]
        return carry

    def add_returned(m, carry):
        for e, z, shift, side in ((0, 0, half, lo_side), (1, top, 0, hi_side)):
            at = pl.ds(z * nx, nx)
            u, k = u_ref[m + shift, z].astype(f32), k_ref[m + shift, z].astype(f32)
            lost = jnp.where(side, expand(ret[e, m]), half_step * k * u)
            pred[m + shift, at] = pred[m + shift, at] - lost
        return carry

    def finish_returned(i):
        wait_recv_pair(returns[i])
        lax.fori_loop(i * share, (i + 1) * share, add_returned, 0)

    gate_wait(rounds - 1)
    scatter = []
    for d in range(1, n_s):
        src = pieces.at[lax.rem(me_s + d, n_s)]
        scatter.append(send(src, parts.at[d], send_s.at[d], recv_s.at[d], space_peer(d)))
    for i in range(LATE, PARTS):
        start_pair(bulks[i])
    for i in range(FIRST, LATE):
        border(i)
    for i in range(FIRST, FIRST + MIDDLE):
        start_pair(returns[i])
    for copy in params_copies:
        copy.wait()
    everyones = all_params[...].reshape(members, -1)
    centre = jnp.sum(everyones, axis=0, keepdims=True) / members
    anomaly[...] = (everyones - centre) / scale
    for i in range(ADDED):
        lax.fori_loop(i * share, (i + 1) * share, add_flux, 0)
    acc = pieces[me_s]
    for d in range(1, n_s):
        scatter[d - 1].wait()
        acc += parts[d]
    total[...] = acc
    sums[me_s] = acc
    gather = [
        send(total, sums.at[me_s], send_g.at[d], recv_g.at[d], space_peer(d))
        for d in range(1, n_s)
    ]
    for i in range(FIRST + MIDDLE, LATE):
        start_pair(returns[i])
    for i in range(LATE, PARTS):
        border(i)
        start_pair(returns[i])

    for i in range(ADDED, PARTS):
        lax.fori_loop(i * share, (i + 1) * share, add_flux, 0)
    for i in range(BACK):
        finish_returned(i)
    for copy in gather:
        copy.wait()
    gram = sums[:, :grams].reshape(members, members)
    cross = jnp.concatenate([sums[i, grams : grams + crosses] for i in range(n_s)], axis=0)
    weights = solve(gram, cross, work)
    posterior_ref[...] = all_params[me_e] + jnp.dot(
        weights, anomaly[...], precision=HI, preferred_element_type=f32
    )

    for i in range(BACK, PARTS):
        finish_returned(i)

    for pair in [ask, reply] + bulks + returns:
        wait_send_pair(pair)

    def drain(c, carry):
        for d in range(hops):
            hand(d, c).wait_send()
        for d in range(1, hops):
            across(d, c).wait_send()
        return carry

    lax.fori_loop(0, chunks, drain, 0)


def analysis(n_e, n_s, position, count, noise, values, std, params, u, k):
    own, cz, nx, ny = u.shape
    slots = position.shape[0]
    chunks = slots // WIDE
    members = own * n_e
    half = own // 2
    piece = members // n_s + 8 * pl.cdiv(own // n_s, 8)
    vmem = pl.BlockSpec(memory_space=pltpu.VMEM)
    hbm = pl.BlockSpec(memory_space=pltpu.HBM)
    dma = pltpu.SemaphoreType.DMA
    field = (own, cz * nx + PAD, ny)
    layers = pltpu.VMEM((half, nx, ny), u.dtype)
    group = 4
    return pl.pallas_call(
        functools.partial(analysis_kernel, n_e, n_s),
        in_specs=[hbm] * 9,
        out_specs=[vmem, vmem],
        out_shape=[pltpu.VMEM(field, f32), pltpu.VMEM(params.shape, f32)],
        scratch_shapes=[
            pltpu.VMEM(u.shape, u.dtype),
            pltpu.VMEM(k.shape, k.dtype),
            pltpu.VMEM((group, cz, nx + 2 * PAD, ny), f32),
            pltpu.VMEM((group, cz, nx + 2 * PAD, ny), f32),
            pltpu.VMEM((group, cz * nx, ny), f32),
            layers, layers, layers, layers,
            pltpu.VMEM((2, half, nx, ny), f32),
            pltpu.VMEM((2, half, nx, ny), bf16),
            pltpu.VMEM((2, half, nx, ny), bf16),
            pltpu.SMEM((slots,), jnp.int32),
            pltpu.VMEM((1, 1), jnp.int32),
            pltpu.VMEM((1, slots), jnp.int32),
            pltpu.VMEM((own, slots), f32),
            pltpu.VMEM((1, slots), f32),
            pltpu.VMEM((1, slots), f32),
            pltpu.VMEM((2, 1, slots), jnp.int32),
            pltpu.VMEM((2, 2, own, slots), bf16),
            pltpu.VMEM((2, 2, own, slots), bf16),
            pltpu.VMEM((chunks, own, WIDE), f32),
            pltpu.VMEM((n_e, chunks, own, WIDE), f32),
            pltpu.VMEM((n_e,) + params.shape, f32),
            pltpu.VMEM((2, chunks, own, WIDE), f32),
            pltpu.VMEM((members + own, members), f32),
            pltpu.VMEM((n_s, piece, members), f32),
            pltpu.VMEM((n_s, piece, members), f32),
            pltpu.VMEM((piece, members), f32),
            pltpu.VMEM((n_s, piece, members), f32),
            pltpu.VMEM((members + own, members), f32),
            pltpu.VMEM((members, params.shape[1]), f32),
            pltpu.SemaphoreType.REGULAR((max(1, (n_s - 1).bit_length()),)),
            dma((15,)),
        ]
        + [dma((2,))] * 4
        + [dma((PARTS, 4))] * 2
        + [dma((PARTS, 2))] * 2
        + [dma((n_e // 2, chunks))] * 4
        + [dma((n_e,))] * 2
        + [dma((n_s,))] * 4,
        compiler_params=pltpu.CompilerParams(
            collective_id=0,
            has_side_effects=True,
            vmem_limit_bytes=VMEM_BYTES - 4 * math.prod(field) - (512 << 10),
        ),
        name="analysis",
    )(
        position, count.reshape(1, 1), position.reshape(1, -1), noise, values.reshape(1, -1),
        std.reshape(1, -1), params, u, k,
    )


def finish_kernel(pred_ref, post_ref, o_ref, posterior_ref, sem):
    members, cells = o_ref.shape[:2]
    block = members // sem.shape[0]

    def copy_of(i):
        at = pl.ds(i * block, block)
        return pltpu.make_async_copy(pred_ref.at[at, pl.ds(0, cells)], o_ref.at[at], sem.at[i])

    copies = [copy_of(i) for i in range(sem.shape[0])]
    for copy in copies:
        copy.start()
    posterior_ref[...] = post_ref[...]
    for copy in copies:
        copy.wait()


def finish(shape, pred, posterior):
    vmem = pl.BlockSpec(memory_space=pltpu.VMEM)
    flat = (shape[0], shape[1] * shape[2], shape[3])
    pred, posterior = pl.pallas_call(
        finish_kernel,
        in_specs=[vmem, vmem],
        out_specs=[pl.BlockSpec(memory_space=pl.ANY), vmem],
        out_shape=[
            jax.ShapeDtypeStruct(flat, f32),
            jax.ShapeDtypeStruct(posterior.shape, f32),
        ],
        scratch_shapes=[pltpu.SemaphoreType.DMA((16,))],
        compiler_params=pltpu.CompilerParams(vmem_limit_bytes=20 << 20),
        name="finish",
    )(pred, posterior)
    return pred.reshape(shape), posterior


def shards(n_e, n_s, u, k, position, count, values, std, noise, params):
    pred, posterior = analysis(n_e, n_s, position, count, noise, values, std, params, u, k)
    pred, posterior = finish(u.shape, pred, posterior)
    return posterior, pred


def solution(mesh):
    in_specs = (
        P("ens", "space", None, None),
        P("ens", "space", None, None),
        P("space"),
        P("space"),
        P("space"),
        P("space"),
        P("ens", "space"),
        P("ens", "space"),
    )
    out_specs = (P("ens", "space"), P("ens", "space", None, None))
    body = functools.partial(shards, mesh.shape["ens"], mesh.shape["space"])
    return jax.shard_map(body, mesh=mesh, in_specs=in_specs, out_specs=out_specs, check_vma=False)
```

```python
import functools
import math

import jax
import jax.numpy as jnp
from jax import lax
from jax.experimental import pallas as pl
from jax.experimental.pallas import tpu as pltpu
from jax.sharding import PartitionSpec as P

half_step = 0.04
HI = lax.Precision.HIGHEST
MESH = pl.DeviceIdType.MESH
VMEM_BYTES = 67043328
PARTS = 8
EARLY = 1
LATE = 8
FIRST = 1
BEFORE = 2
AHEAD = 4
MIDDLE = 0
ADDED = 6
BACK = 1
PAD = 8
WIDE = 256
f32 = jnp.float32
bf16 = jnp.bfloat16


def squeeze(f):
    p = f * f
    p = p * p
    p = p * p
    return jnp.where(f < 0.0, -p, p).astype(bf16)


def expand(y):
    y = y.astype(f32)
    quarter = lax.rsqrt(lax.rsqrt(jnp.abs(y)))
    root = jnp.where(y == 0.0, 0.0, quarter * lax.rsqrt(quarter))
    return jnp.where(y < 0.0, -root, root)


def pad_rows(fu, fk):
    nx = fu.shape[2] - 2 * PAD
    for f in (fu, fk):
        zero = jnp.zeros(f.shape[:2] + (PAD, f.shape[3]), f32)
        f[:, :, :PAD] = zero
        f[:, :, PAD + nx :] = zero


def stencil(lo, hi, u_ref, k_ref, o_ref, fu, fk, fy):
    cz, nx, ny = u_ref.shape[1:]
    group = fu.shape[0]
    r = lax.broadcasted_iota(jnp.int32, (ny, ny), 0)
    c = lax.broadcasted_iota(jnp.int32, (ny, ny), 1)
    eye, following, previous = r == c, r == c + 1, r + 1 == c
    one = lambda mask: jnp.where(mask, 1.0, 0.0)
    plus = [one(following) + one(eye), one(previous) + one(eye)]
    minus = [one(following) - one(eye), one(previous) - one(eye)]
    plus = jnp.concatenate(plus, axis=1).astype(bf16)
    minus = jnp.concatenate(minus, axis=1).astype(bf16)
    span = 32

    def members(i, carry):
        first = lo + i * group
        for w in range(group):
            ks = k_ref[first + w].reshape(cz * nx, ny)
            us = u_ref[first + w].reshape(cz * nx, ny)
            flux = jnp.dot(ks, plus, preferred_element_type=f32) * jnp.dot(
                us, minus, preferred_element_type=f32
            )
            fy[w] = flux[:, :ny] + flux[:, ny:]
            for z in range(cz):
                fu[w, z, PAD : PAD + nx] = u_ref[first + w, z].astype(f32)
                fk[w, z, PAD : PAD + nx] = k_ref[first + w, z].astype(f32)
        for w in range(group):
            for x in range(0, nx, span):
                at = slice(PAD + x, PAD + x + span)
                after = slice(PAD + x + 1, PAD + x + span + 1)
                before = slice(PAD + x - 1, PAD + x + span - 1)
                below = None
                u, k = fu[w, 0, at], fk[w, 0, at]
                for z in range(cz):
                    total = (k + fk[w, z, after]) * (fu[w, z, after] - u)
                    total += (k + fk[w, z, before]) * (fu[w, z, before] - u)
                    total += fy[w, z * nx + x : z * nx + x + span]
                    if below is not None:
                        total -= below
                    if z < cz - 1:
                        u_next, k_next = fu[w, z + 1, at], fk[w, z + 1, at]
                        below = (k + k_next) * (u_next - u)
                        total += below
                    o_ref[first + w, z * nx + x : z * nx + x + span] = u + half_step * total
                    if z < cz - 1:
                        u, k = u_next, k_next
        return carry

    lax.fori_loop(0, (hi - lo) // group, members, 0)


def solve(gram, cross, work):
    members = gram.shape[1]
    rows = lax.broadcasted_iota(jnp.int32, (members, members), 0)
    cols = lax.broadcasted_iota(jnp.int32, (members, members), 1)
    lane = lax.broadcasted_iota(jnp.int32, (1, members), 1)
    work[:members] = gram + jnp.where(rows == cols, 1.0, 0.0)
    work[members:] = cross

    pivots = 8
    segments = 4
    span = members // segments

    def step(lo, s, carry):
        first = lo + s * pivots
        t = work[lo:]
        here = [lane == first + i for i in range(pivots)]
        columns = [
            jnp.sum(jnp.where(here[i], t, 0.0), axis=1, keepdims=True) for i in range(pivots)
        ]
        rows = [work[pl.ds(first + i, 1), :] for i in range(pivots)]
        corner = [
            [jnp.sum(jnp.where(here[j], rows[i], 0.0), axis=1, keepdims=True) for j in range(pivots)]
            for i in range(pivots)
        ]
        rows = [rows[i] - jnp.where(here[i], 1.0, 0.0) for i in range(pivots)]
        for i in range(pivots):
            inverse = 1.0 / corner[i][i]
            rows[i] = rows[i] * inverse
            for j in range(i + 1, pivots):
                corner[i][j] = corner[i][j] * inverse
            for l in range(i + 1, pivots):
                rows[l] = rows[l] - corner[l][i] * rows[i]
                for j in range(i + 1, pivots):
                    corner[l][j] = corner[l][j] - corner[l][i] * corner[i][j]
        for i in range(pivots - 1, -1, -1):
            for j in range(i + 1, pivots):
                rows[i] = rows[i] - corner[i][j] * rows[j]
        for i in range(pivots):
            t = t - columns[i] * rows[i]
        work[lo:] = t
        return carry

    for part in range(segments):
        lax.fori_loop(0, span // pivots, functools.partial(step, part * span), 0)
    return work[members:]


def analysis_kernel(
    n_e, n_s, pos_hbm, count_hbm, slots_hbm, noise_hbm, values_hbm, std_hbm, params_hbm,
    u_hbm, k_hbm,
    pred, posterior_ref,
    u_ref, k_ref, fu, fk, fy, ulo, klo, uhi, khi, flux, back, ret,
    pos_ref, count_ref, slots_ref, noise_ref, values_ref, std_ref, asked, answer, got, picked, all_picked,
    all_params, own_at, part, pieces, parts, total, sums, work, anomaly,
    gate, load, send_q, recv_q, send_w, recv_w, send_b, recv_b, send_r, recv_r,
    send_a, recv_a, send_h, recv_h, send_p, recv_p, send_s, recv_s, send_g, recv_g,
):
    own, cz, nx, ny = u_ref.shape
    slots = slots_ref.shape[1]
    chunks = slots // WIDE
    members = own * n_e
    half = own // 2
    share = half // PARTS
    top = cz - 1
    me_e, me_s = lax.axis_index("ens"), lax.axis_index("space")
    scale = math.sqrt(members - 1.0)
    lo_side, hi_side = me_s > 0, me_s < n_s - 1

    def local(src, dst, i):
        copy = pltpu.make_async_copy(src, dst, load.at[i])
        copy.start()
        return copy

    quarter = own // 4
    loads = []
    for i in range(4):
        at = pl.ds(i * quarter, quarter)
        loads.append(local(u_hbm.at[at], u_ref.at[at], 2 * i))
        loads.append(local(k_hbm.at[at], k_ref.at[at], 2 * i + 1))
    small = [
        local(slots_hbm, slots_ref, 8),
        local(pos_hbm, pos_ref, 13),
        local(count_hbm, count_ref, 14),
        local(noise_hbm, noise_ref, 9),
        local(values_hbm, values_ref, 10),
        local(std_hbm, std_ref, 11),
        local(params_hbm, all_params.at[me_e], 12),
    ]

    def ens_peer(d):
        return (lax.rem(me_e + d, n_e), me_s)

    def space_peer(d):
        return (me_e, lax.rem(me_s + d, n_s))

    barrier = pltpu.get_barrier_semaphore()
    for d in range(1, n_e):
        pl.semaphore_signal(barrier, inc=1, device_id=ens_peer(d), device_id_type=MESH)

    def at_distance(d, what):
        for there, peer in ((me_s >= d, me_s - d), (me_s + d < n_s, me_s + d)):
            @pl.when(there)
            def _():
                what((me_e, peer))

    def signal(sem, peer):
        pl.semaphore_signal(sem, inc=1, device_id=peer, device_id_type=MESH)

    at_distance(1, functools.partial(signal, barrier))
    pad_rows(fu, fk)
    def peers_at(d):
        return (me_s >= d).astype(jnp.int32) + (me_s + d < n_s).astype(jnp.int32)

    pl.semaphore_wait(barrier, n_e - 1 + peers_at(1))

    def gate_signal(r):
        at_distance(1 << r, functools.partial(signal, gate.at[r]))

    def gate_wait(r):
        pl.semaphore_wait(gate.at[r], peers_at(1 << r))

    rounds = gate.shape[0]
    gate_signal(0)

    def remote(src, dst, ssem, rsem, peer):
        return pltpu.make_async_remote_copy(
            src_ref=src, dst_ref=dst, send_sem=ssem, recv_sem=rsem,
            device_id=peer, device_id_type=MESH,
        )

    def send(*args):
        copy = remote(*args)
        copy.start()
        return copy

    above, under = (me_e, lax.rem(me_s + 1, n_s)), (me_e, lax.rem(me_s + n_s - 1, n_s))

    def on_sides(sides, pair, what):
        for side, copies in zip(sides, pair):
            @pl.when(side)
            def _():
                for copy in copies:
                    getattr(copy, what)()

    def start_pair(pair):
        on_sides((hi_side, lo_side), pair, "start")

    def wait_send_pair(pair):
        on_sides((hi_side, lo_side), pair, "wait_send")

    def wait_recv_pair(pair):
        on_sides((lo_side, hi_side), pair, "wait_recv")

    ask = (
        [remote(slots_hbm, asked.at[0], send_q.at[0], recv_q.at[0], above)],
        [remote(slots_hbm, asked.at[1], send_q.at[1], recv_q.at[1], under)],
    )
    start_pair(ask)

    def bulk(i):
        at, src_up, src_down = (
            pl.ds(i * share, share), pl.ds(i * share, share), pl.ds(half + i * share, share)
        )
        s, r = send_b.at[i], recv_b.at[i]
        return (
            [
                remote(u_hbm.at[src_up, top], ulo.at[at], s.at[0], r.at[0], above),
                remote(k_hbm.at[src_up, top], klo.at[at], s.at[1], r.at[1], above),
            ],
            [
                remote(u_hbm.at[src_down, 0], uhi.at[at], s.at[2], r.at[2], under),
                remote(k_hbm.at[src_down, 0], khi.at[at], s.at[3], r.at[3], under),
            ],
        )

    def returned(i):
        at = pl.ds(i * share, share)
        s, r = send_r.at[i], recv_r.at[i]
        return (
            [remote(back.at[1, at], ret.at[0, at], s.at[0], r.at[0], above)],
            [remote(back.at[0, at], ret.at[1, at], s.at[1], r.at[1], under)],
        )

    bulks = [bulk(i) for i in range(PARTS)]
    returns = [returned(i) for i in range(PARTS)]

    def border(i):
        wait_recv_pair(bulks[i])

        def one(m, carry):
            for e, z, shift, un_ref, kn_ref, side in (
                (0, 0, 0, ulo, klo, lo_side), (1, top, half, uhi, khi, hi_side),
            ):
                un = jnp.where(side, un_ref[m].astype(f32), 0.0)
                kn = jnp.where(side, kn_ref[m].astype(f32), 0.0)
                u, k = u_ref[m + shift, z].astype(f32), k_ref[m + shift, z].astype(f32)
                value = half_step * (k + kn) * (un - u)
                flux[e, m] = value
                back[e, m] = squeeze(value)
            return carry

        lax.fori_loop(i * share, (i + 1) * share, one, 0)

    for i in range(EARLY):
        start_pair(bulks[i])
    params_copies = [
        send(params_hbm, all_params.at[me_e], send_p.at[d], recv_p.at[d], ens_peer(d))
        for d in range(1, n_e)
    ]

    def quarter_stencil(i):
        stencil(i * quarter, (i + 1) * quarter, u_ref, k_ref, pred, fu, fk, fy)

    for i in range(BEFORE):
        for copy in loads[2 * i : 2 * i + 2]:
            copy.wait()
        quarter_stencil(i)
    for copy in loads[2 * BEFORE :] + small:
        copy.wait()
    gate_wait(0)

    deep_row = lax.broadcasted_iota(jnp.int32, (2 * ny, WIDE), 0)
    x_row = lax.broadcasted_iota(jnp.int32, (nx, WIDE), 0)
    bits_y, bits_x = int(math.log2(ny)), int(math.log2(nx))

    def coordinates(p):
        y = p & (ny - 1)
        x = lax.shift_right_logical(p, bits_y) & (nx - 1)
        return y, x, lax.shift_right_logical(p, bits_y + bits_x)

    def columns(c):
        return pl.ds(pl.multiple_of(c * WIDE, WIDE), WIDE)

    def pick(layer, hot, mask):
        lines = layer.shape[1]
        g = jnp.dot(layer.reshape(own * lines, 2 * ny), hot, preferred_element_type=f32)
        return jnp.sum(jnp.where(mask, g.reshape(own, lines, WIDE), 0.0), axis=1)

    reply = (
        [remote(answer.at[1], got.at[0], send_w.at[0], recv_w.at[0], above)],
        [remote(answer.at[0], got.at[1], send_w.at[1], recv_w.at[1], under)],
    )
    wait_recv_pair(ask)
    for e, z in ((1, top), (0, 0)):
        def answer_chunk(c, carry):
            at = columns(c)
            y, x, _ = coordinates(asked[e, :, at])
            spot = jnp.where(x < nx // 2, y, y + ny)
            hot = jnp.where(deep_row == spot, 1.0, 0.0).astype(bf16)
            mask = (x_row[: nx // 2] == (x & (nx // 2 - 1)))[None]
            for f, ref in enumerate((u_ref, k_ref)):
                layer = jnp.concatenate([ref[:, z, : nx // 2], ref[:, z, nx // 2 :]], axis=2)
                answer[e, f, :, at] = pick(layer, hot, mask).astype(bf16)
            return carry

        lax.fori_loop(0, chunks, answer_chunk, 0)

        @pl.when((lo_side, hi_side)[e])
        def _():
            reply[1 - e][0].start()

    for i in range(EARLY, LATE):
        start_pair(bulks[i])
    for r in range(1, rounds):
        gate_signal(r)
        if r < rounds - 1:
            gate_wait(r)
    for i in range(BEFORE, 4):
        quarter_stencil(i)
    for i in range(FIRST):
        border(i)
        start_pair(returns[i])

    lane = lax.broadcasted_iota(jnp.int32, (own, ny), 1)
    rows = pred.shape[1]
    flat = pred.reshape(own * rows, ny)
    pair = me_e + 1 - 2 * lax.rem(me_e, 2)
    partner = (pair, me_s)
    hops = n_e // 2

    def hand(d, c):
        block = all_picked.at[lax.rem(me_e + n_e - 2 * d, n_e), c]
        src = picked.at[c] if d == 0 else block
        return remote(src, block, send_h.at[d, c], recv_h.at[d, c], partner)

    def across(d, c):
        dst = all_picked.at[me_e, c]
        return remote(picked.at[c], dst, send_a.at[d, c], recv_a.at[d, c], ens_peer(2 * d))

    def relay(c):
        for d in range(1, hops):
            across(d, c).wait_recv()
            hand(d, c).start()

    def reading(c):
        y, x, z = coordinates(slots_ref[:, columns(c)])
        spot = jnp.where(z == 0, y, jnp.where(z == top, y + ny, -1))
        hot = jnp.where(deep_row == spot, 1.0, 0.0).astype(bf16)
        mask = (x_row == x)[None]
        for f, ref in enumerate((u_ref, k_ref)):
            layer = jnp.concatenate([ref[:, 0], ref[:, top]], axis=2)
            own_at[f, c] = pick(layer, hot, mask)
        for h in range(0, WIDE, ny):
            def step(s, acc):
                for i in range(unroll):
                    jj = s * unroll + i
                    p = pos_ref[c * WIDE + h + jj]
                    v = flat[pl.ds(lax.shift_right_logical(p, bits_y), own, stride=rows), :]
                    v = pltpu.roll(v, (jj - p) & (ny - 1), 1)
                    acc = jnp.where(lane == jj, v, acc)
                return acc

            unroll = ny // 2
            acc = lax.fori_loop(0, ny // unroll, step, jnp.zeros((own, ny), f32))
            picked[c, :, h : h + ny] = acc

    def complete(c):
        at = columns(c)
        _, _, z = coordinates(slots_ref[:, at])
        u_at, k_at = own_at[0, c], own_at[1, c]
        value = picked[c]
        for e, here, side in ((0, z == 0, lo_side), (1, z == top, hi_side)):
            other = jnp.logical_and(here, side)
            u_n = jnp.where(other, got[e, 0, :, at].astype(f32), 0.0)
            k_n = jnp.where(other, got[e, 1, :, at].astype(f32), 0.0)
            value += jnp.where(here, half_step * (k_at + k_n) * (u_n - u_at), 0.0)
        picked[c] = value
        all_picked[me_e, c] = value
        hand(0, c).start()
        for d in range(1, hops):
            across(d, c).start()

    ahead = min(AHEAD, chunks)

    def first_readings(c, carry):
        reading(c)
        return carry

    lax.fori_loop(0, ahead, first_readings, 0)
    wait_recv_pair(reply)

    def more_readings(c, carry):
        reading(c + ahead)
        complete(c)

        @pl.when(c > 0)
        def _():
            relay(c - 1)

        return carry

    lax.fori_loop(0, chunks - ahead, more_readings, 0)
    def last_readings(c, carry):
        complete(c)

        @pl.when(c > 0)
        def _():
            relay(c - 1)

        return carry

    lax.fori_loop(chunks - ahead, chunks, last_readings, 0)
    relay(chunks - 1)

    part[...] = jnp.zeros_like(part)

    def product(c, carry):
        at = columns(c)
        for d in range(hops):
            hand(d, c).wait_recv()
        mine = picked[c]
        live = lax.broadcasted_iota(jnp.int32, (1, WIDE), 1) + c * WIDE < count_ref[...]
        std = std_ref[:, at]
        inverse = jnp.where(live, 1.0 / (std * scale), 0.0)
        misfit = jnp.where(live, (values_ref[:, at] - mine) / std + noise_ref[:, at], 0.0)
        everyone = all_picked[:, c].reshape(members, WIDE)
        centre = jnp.sum(everyone, axis=0, keepdims=True) / members
        spread = (everyone - centre) * inverse
        left = jnp.concatenate([spread, misfit], axis=0)
        part[...] += lax.dot_general(
            left, spread, (((1,), (1,)), ((), ())),
            precision=HI, preferred_element_type=f32,
        )
        return carry

    lax.fori_loop(0, chunks, product, 0)
    grams, crosses = members // n_s, own // n_s
    pieces[:, :grams] = part[:members].reshape(n_s, grams, members)
    for i in range(n_s):
        pieces[i, grams : grams + crosses] = part[members + i * crosses : members + (i + 1) * crosses]
    def add_flux(m, carry):
        bottom, upper = pl.ds(0, nx), pl.ds(top * nx, nx)
        pred[m, bottom] = pred[m, bottom] + flux[0, m]
        pred[m + half, upper] = pred[m + half, upper] + flux[1, m]
        return carry

    def add_returned(m, carry):
        for e, z, shift, side in ((0, 0, half, lo_side), (1, top, 0, hi_side)):
            at = pl.ds(z * nx, nx)
            u, k = u_ref[m + shift, z].astype(f32), k_ref[m + shift, z].astype(f32)
            lost = jnp.where(side, expand(ret[e, m]), half_step * k * u)
            pred[m + shift, at] = pred[m + shift, at] - lost
        return carry

    def finish_returned(i):
        wait_recv_pair(returns[i])
        lax.fori_loop(i * share, (i + 1) * share, add_returned, 0)

    gate_wait(rounds - 1)
    scatter = []
    for d in range(1, n_s):
        src = pieces.at[lax.rem(me_s + d, n_s)]
        scatter.append(send(src, parts.at[d], send_s.at[d], recv_s.at[d], space_peer(d)))
    for i in range(LATE, PARTS):
        start_pair(bulks[i])
    for i in range(FIRST, LATE):
        border(i)
    for i in range(FIRST, FIRST + MIDDLE):
        start_pair(returns[i])
    for copy in params_copies:
        copy.wait()
    everyones = all_params[...].reshape(members, -1)
    centre = jnp.sum(everyones, axis=0, keepdims=True) / members
    anomaly[...] = (everyones - centre) / scale
    for i in range(ADDED):
        lax.fori_loop(i * share, (i + 1) * share, add_flux, 0)
    acc = pieces[me_s]
    for d in range(1, n_s):
        scatter[d - 1].wait()
        acc += parts[d]
    total[...] = acc
    sums[me_s] = acc
    gather = [
        send(total, sums.at[me_s], send_g.at[d], recv_g.at[d], space_peer(d))
        for d in range(1, n_s)
    ]
    for i in range(FIRST + MIDDLE, LATE):
        start_pair(returns[i])
    for i in range(LATE, PARTS):
        border(i)
        start_pair(returns[i])

    for i in range(ADDED, PARTS):
        lax.fori_loop(i * share, (i + 1) * share, add_flux, 0)
    for i in range(BACK):
        finish_returned(i)
    for copy in gather:
        copy.wait()
    gram = sums[:, :grams].reshape(members, members)
    cross = jnp.concatenate([sums[i, grams : grams + crosses] for i in range(n_s)], axis=0)
    weights = solve(gram, cross, work)
    posterior_ref[...] = all_params[me_e] + jnp.dot(
        weights, anomaly[...], precision=HI, preferred_element_type=f32
    )

    for i in range(BACK, PARTS):
        finish_returned(i)

    for pair in [ask, reply] + bulks + returns:
        wait_send_pair(pair)

    def drain(c, carry):
        for d in range(hops):
            hand(d, c).wait_send()
        for d in range(1, hops):
            across(d, c).wait_send()
        return carry

    lax.fori_loop(0, chunks, drain, 0)


def analysis(n_e, n_s, position, count, noise, values, std, params, u, k):
    own, cz, nx, ny = u.shape
    slots = position.shape[0]
    chunks = slots // WIDE
    members = own * n_e
    half = own // 2
    piece = members // n_s + 8 * pl.cdiv(own // n_s, 8)
    vmem = pl.BlockSpec(memory_space=pltpu.VMEM)
    hbm = pl.BlockSpec(memory_space=pltpu.HBM)
    dma = pltpu.SemaphoreType.DMA
    field = (own, cz * nx + PAD, ny)
    layers = pltpu.VMEM((half, nx, ny), u.dtype)
    group = 4
    return pl.pallas_call(
        functools.partial(analysis_kernel, n_e, n_s),
        in_specs=[hbm] * 9,
        out_specs=[vmem, vmem],
        out_shape=[pltpu.VMEM(field, f32), pltpu.VMEM(params.shape, f32)],
        scratch_shapes=[
            pltpu.VMEM(u.shape, u.dtype),
            pltpu.VMEM(k.shape, k.dtype),
            pltpu.VMEM((group, cz, nx + 2 * PAD, ny), f32),
            pltpu.VMEM((group, cz, nx + 2 * PAD, ny), f32),
            pltpu.VMEM((group, cz * nx, ny), f32),
            layers, layers, layers, layers,
            pltpu.VMEM((2, half, nx, ny), f32),
            pltpu.VMEM((2, half, nx, ny), bf16),
            pltpu.VMEM((2, half, nx, ny), bf16),
            pltpu.SMEM((slots,), jnp.int32),
            pltpu.VMEM((1, 1), jnp.int32),
            pltpu.VMEM((1, slots), jnp.int32),
            pltpu.VMEM((own, slots), f32),
            pltpu.VMEM((1, slots), f32),
            pltpu.VMEM((1, slots), f32),
            pltpu.VMEM((2, 1, slots), jnp.int32),
            pltpu.VMEM((2, 2, own, slots), bf16),
            pltpu.VMEM((2, 2, own, slots), bf16),
            pltpu.VMEM((chunks, own, WIDE), f32),
            pltpu.VMEM((n_e, chunks, own, WIDE), f32),
            pltpu.VMEM((n_e,) + params.shape, f32),
            pltpu.VMEM((2, chunks, own, WIDE), f32),
            pltpu.VMEM((members + own, members), f32),
            pltpu.VMEM((n_s, piece, members), f32),
            pltpu.VMEM((n_s, piece, members), f32),
            pltpu.VMEM((piece, members), f32),
            pltpu.VMEM((n_s, piece, members), f32),
            pltpu.VMEM((members + own, members), f32),
            pltpu.VMEM((members, params.shape[1]), f32),
            pltpu.SemaphoreType.REGULAR((max(1, (n_s - 1).bit_length()),)),
            dma((15,)),
        ]
        + [dma((2,))] * 4
        + [dma((PARTS, 4))] * 2
        + [dma((PARTS, 2))] * 2
        + [dma((n_e // 2, chunks))] * 4
        + [dma((n_e,))] * 2
        + [dma((n_s,))] * 4,
        compiler_params=pltpu.CompilerParams(
            collective_id=0,
            has_side_effects=True,
            vmem_limit_bytes=VMEM_BYTES - 4 * math.prod(field) - (512 << 10),
        ),
        name="analysis",
    )(
        position, count.reshape(1, 1), position.reshape(1, -1), noise, values.reshape(1, -1),
        std.reshape(1, -1), params, u, k,
    )


def finish_kernel(pred_ref, post_ref, o_ref, posterior_ref, sem):
    members, cells = o_ref.shape[:2]
    block = members // sem.shape[0]

    def copy_of(i):
        at = pl.ds(i * block, block)
        return pltpu.make_async_copy(pred_ref.at[at, pl.ds(0, cells)], o_ref.at[at], sem.at[i])

    copies = [copy_of(i) for i in range(sem.shape[0])]
    for copy in copies:
        copy.start()
    posterior_ref[...] = post_ref[...]
    for copy in copies:
        copy.wait()


def finish(shape, pred, posterior):
    vmem = pl.BlockSpec(memory_space=pltpu.VMEM)
    flat = (shape[0], shape[1] * shape[2], shape[3])
    pred, posterior = pl.pallas_call(
        finish_kernel,
        in_specs=[vmem, vmem],
        out_specs=[pl.BlockSpec(memory_space=pl.ANY), vmem],
        out_shape=[
            jax.ShapeDtypeStruct(flat, f32),
            jax.ShapeDtypeStruct(posterior.shape, f32),
        ],
        scratch_shapes=[pltpu.SemaphoreType.DMA((16,))],
        compiler_params=pltpu.CompilerParams(vmem_limit_bytes=20 << 20),
        name="finish",
    )(pred, posterior)
    return pred.reshape(shape), posterior


def shards(n_e, n_s, u, k, position, count, values, std, noise, params):
    pred, posterior = analysis(n_e, n_s, position, count, noise, values, std, params, u, k)
    pred, posterior = finish(u.shape, pred, posterior)
    return posterior, pred


def solution(mesh):
    in_specs = (
        P("ens", "space", None, None),
        P("ens", "space", None, None),
        P("space"),
        P("space"),
        P("space"),
        P("space"),
        P("ens", "space"),
        P("ens", "space"),
    )
    out_specs = (P("ens", "space"), P("ens", "space", None, None))
    body = functools.partial(shards, mesh.shape["ens"], mesh.shape["space"])
    return jax.shard_map(body, mesh=mesh, in_specs=in_specs, out_specs=out_specs, check_vma=False)
```
